32 devices in a mesh: layer: 2 (over core), feat: 4 (over y, x), seq: 4 (over z).
Axes of the slice: x: 2, y: 2, z: 4, core: 2. Of those that a mesh axis runs over, the one named last changes fastest.
Arguments:
- mlp_inputs: bfloat16 [2, 768, 2304], P('layer', 'seq'), may hold values from -6 to 6
- enc_weight: bfloat16 [2, 2304, 4096], P('layer', 'seq', 'feat'), may hold values from -0.125 to 0.125
- enc_bias: float32 [2, 4096], P('layer', 'feat'), may hold values from -3 to 3
- dec_weight: bfloat16 [2, 4096, 2304], P('layer', 'feat', 'seq'), may hold values from -0.1875 to 0.1875
- dec_cross: bfloat16 [4096, 2304], P('feat', ('layer', 'seq')), may hold values from -0.1875 to 0.1875
- dec_bias: float32 [2, 2304], P('layer', 'feat'), may hold values from -3 to 3
Outputs:
- recon: bfloat16 [2, 768, 2304], P('layer', 'seq', 'feat')
The draws below stay inside these ranges and needn't reach their ends.
All inputs are finite; a program needn't handle non-finite values.
Results may differ from the reference program's by a relative error of at most 0.0047.
Values may be sent and summed in bfloat16 or wider, within the bound.
A program may use at most 64 MiB of HBM per device.

```python
import jax
import jax.numpy as jnp

D = 2304
F = 4096
TOKENS = 768


def spiked(result, own_key, source, target, blocks, factor):
    owner, partner = [(jnp.arange(result.shape[dim]) // (result.shape[dim] // blocks)).reshape([-1 if axis == dim else 1 for axis in range(result.ndim)]) for dim in (source, target)]
    chosen = jax.random.permutation(own_key, blocks)[partner]
    strong = (owner == chosen) | (owner == (partner + blocks // 2) % blocks)
    return jnp.where(strong, factor * result, result)


def level_of(own_key, shape, cuts, smallest, largest):
    loudness, own = 1.0, jax.random.fold_in(own_key, 6)
    for dim, parts in cuts:
        steps = jnp.exp(jax.random.uniform(jax.random.fold_in(own, dim), (parts,), jnp.float32, smallest / len(cuts), largest / len(cuts)))
        loudness = loudness * jnp.repeat(steps, shape[dim] // parts).reshape([-1 if axis == dim else 1 for axis in range(len(shape))])
    return loudness


def noise(key, dims, deviation, limit, pieces=(), kind=jnp.bfloat16):
    values = jax.random.normal(key, dims, jnp.float32) * deviation
    if len(pieces) > 0:
        values = level_of(key, dims, pieces, -0.22, 0.18) * values
    return jnp.clip(values, min=-limit, max=limit).astype(kind)


def noise_with(own_key, shape, scale, reach, split, heavy, dtype=jnp.bfloat16):
    entries = scale * jax.random.normal(own_key, shape, jnp.float32)
    if split:
        entries = entries * level_of(own_key, shape, split, -0.22, 0.18)
    return jnp.clip(spiked(entries, jax.random.fold_in(own_key, 3), *heavy), -reach, reach).astype(dtype)


def setup_inputs(seed: int = 0) -> dict:
    key_of = jax.random.split(jax.random.key(seed), 7)
    return {
        "mlp_inputs": noise(key_of[0], (2, TOKENS, D), 1.0, 6.0, ((0, 2), (1, 4))),
        "enc_weight": noise(key_of[1], (2, D, F), D ** -0.5, 0.125, ((0, 2), (1, 4), (2, 4))),
        "enc_bias": noise(key_of[2], (2, F), 0.5, 3.0, ((0, 2), (1, 4)), jnp.float32),
        "dec_weight": noise_with(key_of[3], (2, F, D), (F // 2) ** -0.5, 0.1875, ((0, 2), (1, 4), (2, 4)), (1, 2, 4, 2.0)),
        "dec_cross": noise_with(key_of[4], (F, D), (F // 2) ** -0.5, 0.1875, ((0, 4), (1, 8)), (0, 1, 8, 2.0)),
        "dec_bias": noise(key_of[5], (2, D), 0.5, 3.0, ((0, 2), (1, 4)), jnp.float32),
    }


def reference(mlp_inputs, enc_weight, enc_bias, dec_weight, dec_cross, dec_bias):
    first = jnp.dot(mlp_inputs[0], enc_weight[0], preferred_element_type=jnp.float32) + enc_bias[0]
    first = jnp.maximum(first, 0.0).astype(jnp.bfloat16)
    second = jnp.dot(mlp_inputs[1], enc_weight[1], preferred_element_type=jnp.float32) + enc_bias[1]
    second = jnp.maximum(second, 0.0).astype(jnp.bfloat16)
    own_first = jnp.dot(first, dec_weight[0], preferred_element_type=jnp.float32)
    own_second = jnp.dot(second, dec_weight[1], preferred_element_type=jnp.float32)
    cross_terms = jnp.dot(first, dec_cross, preferred_element_type=jnp.float32)
    recon_first = (own_first + dec_bias[0]).astype(jnp.bfloat16)
    recon_second = (own_second + cross_terms + dec_bias[1]).astype(jnp.bfloat16)
    return jnp.stack([recon_first, recon_second], axis=0)
```

```python
import functools

import jax
import jax.numpy as jnp
from jax import lax
from jax.experimental import pallas as pl
from jax.experimental.pallas import tpu as pltpu
from jax.sharding import PartitionSpec as P

MESH = pl.DeviceIdType.MESH
F32, BF16 = jnp.float32, jnp.bfloat16


def passed_along(x, axis, by):
    devices = lax.axis_size(axis)
    pairs = [(i, i + by) for i in range(devices) if 0 <= i + by < devices]
    return lax.ppermute(x, axis, pairs)


def per_device(mlp_inputs, enc_weight, enc_bias, dec_weight, dec_cross, dec_bias):
    token_rows = mlp_inputs[0]
    layer_index = lax.axis_index("layer")
    pre_acts = jnp.dot(
        token_rows,
        lax.all_gather(enc_weight[0], "seq", axis=0, tiled=True),
        preferred_element_type=F32,
    )
    features = jnp.maximum(pre_acts + enc_bias[0], 0.0).astype(BF16)
    own_terms = jnp.dot(
        features,
        lax.all_gather(dec_weight[0], "seq", axis=1, tiled=True),
        preferred_element_type=F32,
    )
    half_rows = features.shape[0] // 2
    sent_half = passed_along(features[half_rows:], "layer", 1)
    cross_input = jnp.where(layer_index == 0, features[:half_rows], sent_half)
    cross_terms = jnp.dot(
        cross_input,
        lax.all_gather(dec_cross, ("layer", "seq"), axis=1, tiled=True),
        preferred_element_type=F32,
    )
    own_sums, cross_sums = (
        lax.psum_scatter(own_terms, "feat", scatter_dimension=1, tiled=True),
        lax.psum_scatter(cross_terms, "feat", scatter_dimension=1, tiled=True),
    )
    moved_sums = passed_along(cross_sums, "layer", 1)
    cross_full = jnp.concatenate([moved_sums, cross_sums], axis=0)
    total = own_sums + dec_bias[0] + jnp.where(layer_index == 1, cross_full, 0.0)
    return total.astype(BF16)[None]


UNIT = 16
COL_CUTS = 2
LINE = 4
OWN_LAG, FWD_LAG, DEC_LAG, SUM_LAG = 3, 6, 8, 5
AHEAD = 2


def decoded(features, columns):
    return lax.dot_general(features, columns, (((1,), (1,)), ((), ())), preferred_element_type=F32)


def kernel(
    n, x_hbm, enc_hbm, encb_ref, dec_hbm, cross_hbm, decb_ref, out_ref,
    xv, enc_ref, dec_ref, cross_ref, xsend, xall, pf, psend, prec, qsend, qrec, feats,
    oown, osend, orecv, csend, crecv, rsum, crs, fin, fcr,
    ld_sem, cw_s, cw_r, x1_s, x1_r, x2_s, x2_r, p_s, p_r, q_s, q_r, g_s, g_r, e_s, e_r,
    o_s, o_r, c_s, c_r, f_s, f_r, h_s, h_r,
):
    layer, f, z = lax.axis_index("layer"), lax.axis_index("feat"), lax.axis_index("seq")
    k = enc_ref.shape[0]
    half = cross_hbm.shape[0]
    r = xv.shape[0]
    pieces = r // UNIT
    steps = pieces * n
    wide = enc_ref.shape[1] // COL_CUTS
    mid = n // 2
    hrows = mid * UNIT
    first, second = layer == 0, layer == 1
    side = lax.div(z, mid)
    inner = (z == mid - 1) | (z == mid)
    edge = (z == 0) | (z == n - 1)
    z_edge, z_inner, z_other = side * (n - 1), mid - 1 + side, mid - side
    near = pl.ds(pl.multiple_of(side * hrows, hrows), hrows)
    far = pl.ds(pl.multiple_of((1 - side) * hrows, hrows), hrows)

    def peer(dx):
        total, bit = 0, 1
        while bit < n:
            own = lax.rem(lax.div(f, bit), 2)
            total = total + bit * ((1 - own) if dx & bit else own)
            bit *= 2
        return total

    def order(u):
        return list(range(1, n)) + [0] if u else list(range(n))

    def split(s):
        return s // n, order(s // n)[s % n]

    def cols(c):
        return pl.ds(c * wide, wide)

    def block(t):
        return pl.ds(pl.multiple_of(t * UNIT, UNIT), UNIT)

    pending = []

    def copy(src, dst, ss, rs, to):
        a, b, c = to
        return pltpu.make_async_remote_copy(
            src_ref=src, dst_ref=dst, send_sem=ss, recv_sem=rs,
            device_id={"layer": a, "feat": b, "seq": c}, device_id_type=MESH,
        )

    def on(cond, run):
        if cond is None:
            run()
        else:
            pl.when(cond)(run)

    def send(cond, make):
        on(cond, lambda: make().start())
        pending.append((cond, make))

    def arrive(cond, dst, sem):
        on(cond, lambda: copy(dst, dst, sem, sem, (layer, f, z)).wait_recv())

    def flush():
        for cond, make in pending:
            on(cond, lambda make=make: make().wait_send())
        pending.clear()

    loads = [
        pltpu.make_async_copy(x_hbm.at[pl.ds(pl.multiple_of(f * r, UNIT), r)], xv, ld_sem.at[0]),
        pltpu.make_async_copy(enc_hbm, enc_ref, ld_sem.at[1]),
        pltpu.make_async_copy(cross_hbm, cross_ref.at[pl.ds(0, half)], ld_sem.at[2]),
        pltpu.make_async_copy(dec_hbm, dec_ref, ld_sem.at[3]),
    ]
    for load in loads:
        load.start()

    barrier = pltpu.get_barrier_semaphore()
    greeted = []
    for a in range(n):
        for b in range(n):
            if a or b:
                greeted.append((layer, lax.rem(f + a, n), lax.rem(z + b, n)))
    greeted += [(1 - layer, lax.rem(f + a, n), z) for a in range(n)]
    for a, b, c in greeted:
        pl.semaphore_signal(
            barrier, inc=1, device_id={"layer": a, "feat": b, "seq": c}, device_id_type=MESH
        )

    loads[0].wait()
    for u in range(pieces):
        for t in range(n):
            xsend[u, t] = xv[u * UNIT:(u + 1) * UNIT, t * k:(t + 1) * k]
    pl.semaphore_wait(barrier, len(greeted))
    for u in range(pieces):
        for d in range(n - 1, 0, -1):
            for sign in (1, -1):
                t = z + sign * d
                send((t < n) & (t >= 0), lambda t=t, u=u: copy(
                    xsend.at[u, t], xall.at[u, f, block(z)], x1_s.at[u, t], x1_r.at[u, z], (layer, f, t)))
    for u in range(pieces):
        xall[u, f, block(z), :] = xsend[u, z]
    loads[2].wait()
    send(second, lambda: copy(
        cross_ref.at[pl.ds(0, half)], cross_ref.at[pl.ds(half, half)], cw_s.at[0], cw_r.at[0], (0, f, z)))

    def spread(u):
        for t in range(n):
            arrive(t != z, xall.at[u, f, block(t)], x1_r.at[u, t])
        for dx in range(1, n):
            send(None, lambda dx=dx: copy(
                xall.at[u, f], xall.at[u, f], x2_s.at[u, dx], x2_r.at[u, dx], (layer, peer(dx), z)))

    def encode(s):
        u, dx = split(s)
        p = peer(dx)
        if dx:
            arrive(None, xall.at[u, p], x2_r.at[u, dx])
        pf[s] = jnp.dot(xall[u, p], enc_ref[...], preferred_element_type=F32)

        @pl.when(edge)
        def _():
            psend[s] = pf[s].astype(BF16)
        for c in range(COL_CUTS):
            for part, which in ((far, 0), (near, 1)):
                send(edge, lambda part=part, which=which, c=c: copy(
                    psend.at[s, part, cols(c)], prec.at[s, part, cols(c)],
                    p_s.at[s, c, which], p_r.at[s, c, which], (layer, f, z_inner)))

    def relay(s, c):
        arrive(inner, prec.at[s, far, cols(c)], p_r.at[s, c, 0])

        @pl.when(inner)
        def _():
            qsend[s, :, cols(c)] = (pf[s, far, cols(c)] + prec[s, far, cols(c)].astype(F32)).astype(BF16)
        send(inner, lambda: copy(
            qsend.at[s, :, cols(c)], qrec.at[s, :, cols(c)], q_s.at[s, c], q_r.at[s, c], (layer, f, z_other)))

    def own(s, c):
        arrive(inner, prec.at[s, near, cols(c)], p_r.at[s, c, 1])
        arrive(inner, qrec.at[s, :, cols(c)], q_r.at[s, c])

        @pl.when(inner)
        def _():
            total = pf[s, near, cols(c)] + encb_ref[:, cols(c)]
            total += prec[s, near, cols(c)].astype(F32)
            total += qrec[s, :, cols(c)].astype(F32)
            feats[s, near, cols(c)] = jnp.maximum(total, 0.0).astype(BF16)
        at = lambda: feats.at[s, near, cols(c)]
        send(inner, lambda: copy(at(), at(), g_s.at[s, c], g_r.at[s, c], (layer, f, z_other)))
        send(inner, lambda: copy(at(), at(), e_s.at[s, c, 0], e_r.at[s, c, 0], (layer, f, z_edge)))

    def forward(s, c):
        at = lambda: feats.at[s, far, cols(c)]
        arrive(inner, at(), g_r.at[s, c])
        send(inner, lambda: copy(at(), at(), e_s.at[s, c, 1], e_r.at[s, c, 1], (layer, f, z_edge)))

    def decode(s):
        u, dx = split(s)
        for c in range(COL_CUTS):
            arrive(edge, feats.at[s, near, cols(c)], e_r.at[s, c, 0])
            arrive(edge, feats.at[s, far, cols(c)], e_r.at[s, c, 1])

        def crossed():
            @pl.when(first)
            def _():
                csend[s] = decoded(feats[s], cross_ref[...]).astype(BF16)
            send(first, lambda: copy(
                csend.at[s], crecv.at[s], c_s.at[s], c_r.at[s], (1, peer(dx), z)))

        if not dx:
            crossed()
        terms = decoded(feats[s], dec_ref[...])
        if dx:
            osend[s] = terms.astype(BF16)
            send(None, lambda: copy(
                osend.at[s], orecv.at[s], o_s.at[s], o_r.at[s], (layer, peer(dx), z)))
            crossed()
        else:
            oown[u] = terms

    def summed(u):
        total = oown[u]
        for i in range(n):
            s = u * n + i
            if split(s)[1]:
                arrive(None, orecv.at[s], o_r.at[s])
                total += orecv[s].astype(F32)
        rsum[u] = total.astype(BF16)
        for t in range(n):
            here = (z == t) & (f == z)
            send(jnp.logical_not(here), lambda t=t: copy(
                rsum.at[u, pl.ds(t * UNIT, UNIT)], fin.at[u, f], f_s.at[u, t], f_r.at[u, f], (layer, z, t)))

        @pl.when(f == z)
        def _():
            fin[u, f] = rsum[u, block(z), :]

        for i in range(n):
            s = u * n + i
            arrive(second, crecv.at[s], c_r.at[s])

        @pl.when(second)
        def _():
            sums = crecv[u * n].astype(F32)
            for i in range(1, n):
                sums += crecv[u * n + i].astype(F32)
            for h in range(2):
                crs[u, h] = sums[:, h * half:(h + 1) * half].astype(BF16)
        j = lax.rem(z, 2)
        for h in range(2):
            to = h * mid + lax.div(z, 2)
            for t in range(n):
                here = (z == t) & (f == to)
                send(second & jnp.logical_not(here), lambda h=h, t=t, to=to: copy(
                    crs.at[u, h, pl.ds(t * UNIT, UNIT)], fcr.at[u, j, f],
                    h_s.at[u, h, t], h_r.at[u, j, f], (layer, to, t)))

            @pl.when(second & (f == to))
            def _(h=h):
                fcr[u, j, f] = crs[u, h, block(z), :]

    def finish(u):
        for g in range(n):
            arrive(jnp.logical_not((g == f) & (f == z)), fin.at[u, g], f_r.at[u, g])
            for j in range(2):
                source = lax.rem(f, mid) * 2 + j
                arrive(second & jnp.logical_not((g == f) & (z == source)), fcr.at[u, j, g], h_r.at[u, j, g])
            part = slice(g * r + u * UNIT, g * r + (u + 1) * UNIT)

            @pl.when(first)
            def _():
                out_ref[part] = (fin[u, g].astype(F32) + decb_ref[...]).astype(BF16)

            @pl.when(second)
            def _():
                cross = jnp.concatenate([fcr[u, 0, g].astype(F32), fcr[u, 1, g].astype(F32)], axis=1)
                out_ref[part] = (fin[u, g].astype(F32) + cross + decb_ref[...]).astype(BF16)

    spread(0)
    loads[1].wait()
    encode(0)
    for u in range(1, pieces):
        spread(u)
    for s in range(1, AHEAD):
        encode(s)
    loads[3].wait()
    arrive(first, cross_ref.at[pl.ds(half, half)], cw_r.at[0])
    subs = steps * COL_CUTS
    last = subs - 1 + DEC_LAG
    for q in range(last + 1):
        if q < subs:
            relay(q // COL_CUTS, q % COL_CUTS)
        for lag, run in ((OWN_LAG, own), (FWD_LAG, forward)):
            if 0 <= q - lag < subs:
                run((q - lag) // COL_CUTS, (q - lag) % COL_CUTS)
        if q % COL_CUTS == 0 and AHEAD <= q // COL_CUTS + AHEAD < steps:
            encode(q // COL_CUTS + AHEAD)
        if q >= DEC_LAG and (q - DEC_LAG) % COL_CUTS == COL_CUTS - 1:
            decode((q - DEC_LAG) // COL_CUTS)
        for u in range(pieces - 1):
            if q == min((u + 1) * n * COL_CUTS - 1 + DEC_LAG + SUM_LAG, last - 1):
                summed(u)
    summed(pieces - 1)
    for u in range(pieces - 1):
        finish(u)
    tail = pending[-3 * n:]
    del pending[-3 * n:]
    flush()
    finish(pieces - 1)
    pending.extend(tail)
    flush()


def by_kernel(n, mlp_inputs, enc_weight, enc_bias, dec_weight, dec_cross, dec_bias):
    x, enc, dec, cross = mlp_inputs[0], enc_weight[0], dec_weight[0].T, dec_cross.T
    r = x.shape[0] // n
    k, width = enc.shape
    columns, half = dec.shape[0], cross.shape[0]
    pieces = r // UNIT
    steps, rows = pieces * n, n * UNIT
    vmem = pl.BlockSpec(memory_space=pltpu.VMEM)
    hbm = pl.BlockSpec(memory_space=pl.ANY)
    dma = pltpu.SemaphoreType.DMA
    scratch = [
        pltpu.VMEM((r, x.shape[1]), BF16),
        pltpu.VMEM(enc.shape, BF16),
        pltpu.VMEM(dec.shape, BF16),
        pltpu.VMEM((2 * half, width), BF16),
        pltpu.VMEM((pieces, n, UNIT, k), BF16),
        pltpu.VMEM((pieces, n, rows, k), BF16),
        pltpu.VMEM((steps, rows, width), F32),
        pltpu.VMEM((steps, rows, width), BF16),
        pltpu.VMEM((steps, rows, width), BF16),
        pltpu.VMEM((steps, rows // 2, width), BF16),
        pltpu.VMEM((steps, rows // 2, width), BF16),
        pltpu.VMEM((steps, rows, width), BF16),
        pltpu.VMEM((pieces, rows, columns), F32),
        pltpu.VMEM((steps, rows, columns), BF16),
        pltpu.VMEM((steps, rows, columns), BF16),
        pltpu.VMEM((steps, rows, 2 * half), BF16),
        pltpu.VMEM((steps, rows, 2 * half), BF16),
        pltpu.VMEM((pieces, rows, columns), BF16),
        pltpu.VMEM((pieces, 2, rows, half), BF16),
        pltpu.VMEM((pieces, n, UNIT, columns), BF16),
        pltpu.VMEM((pieces, 2, n, UNIT, half), BF16),
        dma((4,)), dma((1,)), dma((1,)),
        dma((pieces, n)), dma((pieces, n)), dma((pieces, n)), dma((pieces, n)),
        dma((steps, COL_CUTS, 2)), dma((steps, COL_CUTS, 2)),
        dma((steps, COL_CUTS)), dma((steps, COL_CUTS)),
        dma((steps, COL_CUTS)), dma((steps, COL_CUTS)),
        dma((steps, COL_CUTS, 2)), dma((steps, COL_CUTS, 2)),
        dma((steps,)), dma((steps,)), dma((steps,)), dma((steps,)),
        dma((pieces, n)), dma((pieces, n)), dma((pieces, 2, n)), dma((pieces, 2, n)),
    ]
    out = pl.pallas_call(
        functools.partial(kernel, n),
        out_shape=jax.ShapeDtypeStruct((x.shape[0], columns), BF16),
        in_specs=[hbm, hbm, vmem, hbm, hbm, vmem],
        out_specs=vmem,
        scratch_shapes=scratch,
        compiler_params=pltpu.CompilerParams(
            collective_id=0, has_side_effects=True, vmem_limit_bytes=56 * 2**20
        ),
    )(x, enc, enc_bias, dec, cross, dec_bias)
    return out[None]


def solution(mesh):
    placed = (
        P("layer", "seq", None),
        P("layer", "seq", "feat"),
        P("layer", "feat"),
        P("layer", "feat", "seq"),
        P("feat", ("layer", "seq")),
        P("layer", "feat"),
    )
    groups = mesh.shape["feat"]

    def body(mlp_inputs, *rest):
        fits = groups == LINE and mesh.shape["seq"] == LINE and mlp_inputs.shape[1] % (UNIT * groups) == 0
        if fits and mesh.shape["layer"] == 2 and rest[0].shape[2] % (COL_CUTS * 128) == 0:
            return by_kernel(groups, mlp_inputs, *rest)
        return per_device(mlp_inputs, *rest)

    return jax.shard_map(
        body, mesh=mesh, in_specs=placed, out_specs=P("layer", "seq", "feat"), check_vma=False
    )
```

```python
import functools

import jax
import jax.numpy as jnp
from jax import lax
from jax.experimental import pallas as pl
from jax.experimental.pallas import tpu as pltpu
from jax.sharding import PartitionSpec as P

MESH = pl.DeviceIdType.MESH
F32, BF16 = jnp.float32, jnp.bfloat16


def passed_along(x, axis, by):
    devices = lax.axis_size(axis)
    pairs = [(i, i + by) for i in range(devices) if 0 <= i + by < devices]
    return lax.ppermute(x, axis, pairs)


def per_device(mlp_inputs, enc_weight, enc_bias, dec_weight, dec_cross, dec_bias):
    token_rows = mlp_inputs[0]
    layer_index = lax.axis_index("layer")
    pre_acts = jnp.dot(
        token_rows,
        lax.all_gather(enc_weight[0], "seq", axis=0, tiled=True),
        preferred_element_type=F32,
    )
    features = jnp.maximum(pre_acts + enc_bias[0], 0.0).astype(BF16)
    own_terms = jnp.dot(
        features,
        lax.all_gather(dec_weight[0], "seq", axis=1, tiled=True),
        preferred_element_type=F32,
    )
    half_rows = features.shape[0] // 2
    sent_half = passed_along(features[half_rows:], "layer", 1)
    cross_input = jnp.where(layer_index == 0, features[:half_rows], sent_half)
    cross_terms = jnp.dot(
        cross_input,
        lax.all_gather(dec_cross, ("layer", "seq"), axis=1, tiled=True),
        preferred_element_type=F32,
    )
    own_sums, cross_sums = (
        lax.psum_scatter(own_terms, "feat", scatter_dimension=1, tiled=True),
        lax.psum_scatter(cross_terms, "feat", scatter_dimension=1, tiled=True),
    )
    moved_sums = passed_along(cross_sums, "layer", 1)
    cross_full = jnp.concatenate([moved_sums, cross_sums], axis=0)
    total = own_sums + dec_bias[0] + jnp.where(layer_index == 1, cross_full, 0.0)
    return total.astype(BF16)[None]


UNIT = 16
LINE = 4
FINE_IN, FINE_OUT = 2, 2
DIRECT_IN, DIRECT_OUT = 0, 0
STEP_LAGS = {"own": 1.2, "forward": 2.4, "decode": 4.0, "sum": 2.5, "encode": -2.5}
FIRST_PIECE = ((0.01, 0.2), (0.1, 0.3), (0.6, 0.7))
SPREAD = 0.5


def decoded(features, columns):
    return lax.dot_general(features, columns, (((1,), (1,)), ((), ())), preferred_element_type=F32)


def cuts_of(s, steps):
    return 2 if s < FINE_IN or s >= steps - FINE_OUT else 1


def parts_of(steps):
    parts, start = [], []
    for s in range(steps):
        start.append(len(parts))
        parts += [(s, c, cuts_of(s, steps)) for c in range(cuts_of(s, steps))]
    return parts, start


def kernel(
    n, x_hbm, enc_hbm, encb_ref, dec_hbm, cross_hbm, decb_ref, out_ref,
    xv, enc_ref, dec_ref, cross_ref, xsend, xall, pf, psend, prec, drec, qsend, qrec, feats,
    oown, osend, orecv, csend, crecv, rsum, crs, fin, fcr,
    ld_sem, cw_r, x1_r, x2_r, p_r, d_r, q_r, g_r, o_r, c_r, f_r, h_r,
    x1_s, x2_s, f_s, h_s, sent,
):
    layer, f, z = lax.axis_index("layer"), lax.axis_index("feat"), lax.axis_index("seq")
    k = enc_ref.shape[0]
    half = cross_hbm.shape[0]
    r, width = xv.shape[0], enc_ref.shape[1]
    pieces = r // UNIT
    steps = pieces * n
    parts, start = parts_of(steps)
    mid = n // 2
    hrows = mid * UNIT
    first, second = layer == 0, layer == 1
    side = lax.div(z, mid)
    inner = (z == mid - 1) | (z == mid)
    edge = (z == 0) | (z == n - 1)
    z_edge, z_inner, z_other, z_far = side * (n - 1), mid - 1 + side, mid - side, (1 - side) * (n - 1)
    far = pl.ds(pl.multiple_of(side * hrows, hrows), hrows)
    near = pl.ds(pl.multiple_of((1 - side) * hrows, hrows), hrows)

    def peer(dx):
        total, bit = 0, 1
        while bit < n:
            own = lax.rem(lax.div(f, bit), 2)
            total = total + bit * ((1 - own) if dx & bit else own)
            bit *= 2
        return total

    sequence = [(0, dx) for dx in range(n)]
    sequence += [(u, dx) for u in range(1, pieces) for dx in range(n - 1, 0, -1)]
    sequence += [(u, 0) for u in range(1, pieces)]

    def split(s):
        return sequence[s]

    def outgoing(u, dx):
        return u * (n - 1) + dx - 1

    def cols(i):
        _, c, cuts = parts[i]
        return pl.ds(c * (width // cuts), width // cuts)

    def block(t):
        return pl.ds(pl.multiple_of(t * UNIT, UNIT), UNIT)

    def copy(src, dst, ss, rs, to):
        a, b, c = to
        return pltpu.make_async_remote_copy(
            src_ref=src, dst_ref=dst, send_sem=ss, recv_sem=rs,
            device_id={"layer": a, "feat": b, "seq": c}, device_id_type=MESH,
        )

    def on(cond, run):
        if cond is None:
            run()
        else:
            pl.when(cond)(run)

    def send(cond, make):
        on(cond, lambda: make().start())

    def arrive(cond, dst, sem):
        on(cond, lambda: copy(dst, dst, sem, sem, (layer, f, z)).wait_recv())

    def left(cond, src, sem):
        on(cond, lambda: copy(src, src, sem, sem, (layer, f, z)).wait_send())

    turns = [lax.rem(z + d, n) for d in (mid, mid + 1, mid - 1, 0)]
    S_P, S_Q, S_G, S_E, S_O, S_C, S_W = range(7)

    loads = [
        pltpu.make_async_copy(x_hbm.at[pl.ds(pl.multiple_of(f * r, UNIT), r)], xv, ld_sem.at[0]),
        pltpu.make_async_copy(enc_hbm, enc_ref, ld_sem.at[1]),
        pltpu.make_async_copy(cross_hbm, cross_ref.at[pl.ds(0, half)], ld_sem.at[2]),
        pltpu.make_async_copy(dec_hbm, dec_ref, ld_sem.at[3]),
    ]
    for load in loads:
        load.start()

    barrier = pltpu.get_barrier_semaphore()
    greeted = []
    for a in range(n):
        for b in range(n):
            if a or b:
                greeted.append((layer, lax.rem(f + a, n), lax.rem(z + b, n)))
    greeted += [(1 - layer, lax.rem(f + a, n), z) for a in range(n)]
    for a, b, c in greeted:
        pl.semaphore_signal(
            barrier, inc=1, device_id={"layer": a, "feat": b, "seq": c}, device_id_type=MESH
        )

    loads[0].wait()
    for u in range(pieces):
        for t in range(n):
            xsend[u, t] = xv[u * UNIT:(u + 1) * UNIT, t * k:(t + 1) * k]
        if u == 0:
            pl.semaphore_wait(barrier, len(greeted))
        for d in range(n - 1, 0, -1):
            for sign in (1, -1):
                t = z + sign * d
                send((t < n) & (t >= 0), lambda t=t, u=u: copy(
                    xsend.at[u, t], xall.at[u, f, block(z)], x1_s.at[u], x1_r.at[u, lax.rem(side + lax.div(t, mid), 2)], (layer, f, t)))
        xall[u, f, block(z), :] = xsend[u, z]
    loads[2].wait()
    send(second, lambda: copy(
        cross_ref.at[pl.ds(0, half)], cross_ref.at[pl.ds(half, half)], sent.at[S_W], cw_r.at[0], (0, f, z)))

    halves = ((far, 0), (near, 1))

    def spread(u, half):
        part, h = half
        arrive(None, xall.at[u, f, pl.ds(0, (mid - 1 + h) * UNIT)], x1_r.at[u, h])
        for dx in range(1, n):
            send(None, lambda dx=dx: copy(
                xall.at[u, f, part], xall.at[u, f, part], x2_s.at[u], x2_r.at[u, dx, h], (layer, peer(dx), z)))

    def encode(s, chosen):
        u, dx = split(s)
        p = peer(dx)
        if dx:
            for part, h in chosen:
                arrive(None, xall.at[u, p, part], x2_r.at[u, dx, h])
        rows = chosen[0][0] if len(chosen) == 1 else pl.ds(0, 2 * hrows)
        pf[s, rows] = jnp.dot(xall[u, p, rows], enc_ref[...], preferred_element_type=F32)

        @pl.when(edge)
        def _():
            psend[s, rows] = pf[s, rows].astype(BF16)
        for i in range(start[s], start[s] + cuts_of(s, steps)):
            for part, h in chosen:
                at = lambda i=i, part=part: psend.at[s, part, cols(i)]
                if h == 0 and s < DIRECT_IN:
                    send(edge, lambda i=i, at=at: copy(
                        at(), drec.at[s, :, cols(i)], sent.at[S_P], d_r.at[i], (layer, f, z_other)))
                else:
                    send(edge, lambda i=i, at=at, part=part, h=h: copy(
                        at(), prec.at[s, part, cols(i)], sent.at[S_P], p_r.at[i, h], (layer, f, z_inner)))

    def relay(i):
        s = parts[i][0]
        if s >= DIRECT_IN:
            arrive(inner, prec.at[s, far, cols(i)], p_r.at[i, 0])

        @pl.when(inner)
        def _():
            total = pf[s, far, cols(i)]
            if s >= DIRECT_IN:
                total += prec[s, far, cols(i)].astype(F32)
            qsend[s, :, cols(i)] = total.astype(BF16)
        send(inner, lambda: copy(
            qsend.at[s, :, cols(i)], qrec.at[s, :, cols(i)], sent.at[S_Q], q_r.at[i], (layer, f, z_other)))

    def own(i):
        s = parts[i][0]
        arrive(inner, prec.at[s, near, cols(i)], p_r.at[i, 1])
        if s < DIRECT_IN:
            arrive(inner, drec.at[s, :, cols(i)], d_r.at[i])
        arrive(inner, qrec.at[s, :, cols(i)], q_r.at[i])

        @pl.when(inner)
        def _():
            total = pf[s, near, cols(i)] + encb_ref[:, cols(i)]
            total += prec[s, near, cols(i)].astype(F32)
            total += qrec[s, :, cols(i)].astype(F32)
            if s < DIRECT_IN:
                total += drec[s, :, cols(i)].astype(F32)
            feats[s, near, cols(i)] = jnp.maximum(total, 0.0).astype(BF16)
        at = lambda: feats.at[s, near, cols(i)]
        to = [(g_r.at[i], S_G, z_other), (p_r.at[start[s], 0], S_E, z_edge)]
        if s >= steps - DIRECT_OUT:
            to = [(p_r.at[start[s], 0], S_E, z_far)] + to
        for sem, ss, zz in to:
            send(inner, lambda sem=sem, ss=ss, zz=zz: copy(at(), at(), sent.at[ss], sem, (layer, f, zz)))

    def forward(i):
        s = parts[i][0]
        at = lambda: feats.at[s, far, cols(i)]
        arrive(inner, at(), g_r.at[i])
        if s < steps - DIRECT_OUT:
            send(inner, lambda: copy(at(), at(), sent.at[S_E], p_r.at[start[s], 0], (layer, f, z_edge)))

    def decode(s):
        u, dx = split(s)
        arrive(edge, feats.at[s], p_r.at[start[s], 0])

        def crossed():
            @pl.when(first)
            def _():
                csend[u * n + dx] = decoded(feats[s], cross_ref[...]).astype(BF16)
            send(first, lambda: copy(
                csend.at[u * n + dx], crecv.at[u * n + dx], sent.at[S_C], c_r.at[u], (1, peer(dx), z)))

        if not dx:
            crossed()
        terms = decoded(feats[s], dec_ref[...])
        if dx:
            osend[outgoing(u, dx)] = terms.astype(BF16)
            send(None, lambda: copy(
                osend.at[outgoing(u, dx)], orecv.at[outgoing(u, dx)], sent.at[S_O], o_r.at[u], (layer, peer(dx), z)))
            crossed()
        else:
            oown[u] = terms

    def summed(u):
        arrive(None, orecv.at[pl.ds(u * (n - 1), n - 1)], o_r.at[u])
        total = oown[u]
        for dx in range(1, n):
            total += orecv[outgoing(u, dx)].astype(F32)
        rsum[u] = total.astype(BF16)
        for t in turns:
            here = (z == t) & (f == z)
            send(jnp.logical_not(here), lambda t=t: copy(
                rsum.at[u, block(t)], fin.at[u, f], f_s.at[u], f_r.at[u], (layer, z, t)))

        @pl.when(f == z)
        def _():
            fin[u, f] = rsum[u, block(z), :]

    def crossed_sum(u):
        arrive(second, crecv.at[pl.ds(u * n, n)], c_r.at[u])

        @pl.when(second)
        def _():
            sums = crecv[u * n].astype(F32)
            for i in range(1, n):
                sums += crecv[u * n + i].astype(F32)
            for h in range(2):
                crs[u, h] = sums[:, h * half:(h + 1) * half].astype(BF16)
        slot = lax.rem(z, 2) * n + f
        for h in range(2):
            to = h * mid + lax.div(z, 2)
            for t in turns:
                here = (z == t) & (f == to)
                send(second & jnp.logical_not(here), lambda h=h, t=t, to=to: copy(
                    crs.at[u, h, block(t)], fcr.at[u, slot],
                    h_s.at[u], h_r.at[u], (layer, to, t)))

            @pl.when(second & (f == to))
            def _(h=h):
                fcr[u, slot] = crs[u, h, block(z), :]

    own_rows = f == z
    own_cross = lax.rem(f, 2) == lax.div(z, 2)

    def each(run, u, mine, whole, other):
        count = whole.shape[1]
        run(mine, whole.at[u, pl.ds(0, count - 1)], other.at[u])
        rest = jnp.logical_not(mine) if mine is own_rows else second & jnp.logical_not(own_cross)
        run(rest, whole.at[u], other.at[u])

    def finish(u):
        each(arrive, u, own_rows, fin, f_r)
        each(arrive, u, second & own_cross, fcr, h_r)
        for g in range(n):
            part = slice(g * r + u * UNIT, g * r + (u + 1) * UNIT)

            @pl.when(first)
            def _():
                out_ref[part] = (fin[u, g].astype(F32) + decb_ref[...]).astype(BF16)

            @pl.when(second)
            def _():
                cross = jnp.concatenate([fcr[u, g].astype(F32), fcr[u, n + g].astype(F32)], axis=1)
                out_ref[part] = (fin[u, g].astype(F32) + cross + decb_ref[...]).astype(BF16)

    for h in range(2):
        spread(0, halves[h])
        if h == 0:
            loads[1].wait()
        encode(0, halves[h:h + 1])

    events = []

    def place(time, rank, run, *given):
        events.append((time, rank, len(events), run, given))

    for i, (s, c, cuts) in enumerate(parts):
        begin = s + c / cuts
        place(begin, 0, relay, i)
        place(begin + STEP_LAGS["own"], 1, own, i)
        place(begin + STEP_LAGS["forward"], 2, forward, i)
    for dx in range(1, n):
        for h in range(2):
            place(FIRST_PIECE[dx - 1][h], 3, encode, dx, halves[h:h + 1])
    for u in range(1, pieces):
        for h in range(2):
            place(SPREAD * u, 3, spread, u, halves[h])
    last = [max(s for s in range(steps) if split(s)[0] == u) for u in range(pieces)]
    for s in range(steps):
        if s >= n:
            place(s + STEP_LAGS["encode"], 3, encode, s, halves)
        place(s + STEP_LAGS["decode"], 4, decode, s)
    for u in range(pieces):
        late = STEP_LAGS["decode"] + (0 if u else STEP_LAGS["sum"])
        place(last[u] + late, 5, summed, u)
        place(last[u] + late if u == 0 else steps - 1 + late, 6, crossed_sum, u)
    place(steps - 2.5 + STEP_LAGS["decode"], 5, finish, 0)
    place(0.5, 6, loads[3].wait)
    place(0.5, 7, lambda: arrive(first, cross_ref.at[pl.ds(half, half)], cw_r.at[0]))
    for _, _, _, run, given in sorted(events, key=lambda e: e[:3]):
        run(*given)
    for u in range(pieces - 1):
        if u:
            finish(u)
        left(None, xall.at[u, f, pl.ds(0, (n - 1) * UNIT)], x1_s.at[u])
        left(None, xall.at[u, pl.ds(0, n - 1)], x2_s.at[u])
        each(left, u, own_rows, fin, f_s)
        each(left, u, second & own_cross, fcr, h_s)
    u = pieces - 1
    left(None, xall.at[u, f, pl.ds(0, (n - 1) * UNIT)], x1_s.at[u])
    left(None, xall.at[u, pl.ds(0, n - 1)], x2_s.at[u])
    left(edge, psend, sent.at[S_P])
    left(inner, qsend, sent.at[S_Q])
    left(inner, qsend, sent.at[S_G])
    left(inner, feats, sent.at[S_E])
    left(None, osend.at[pl.ds(0, steps - pieces)], sent.at[S_O])
    left(first, csend, sent.at[S_C])
    left(second, cross_ref.at[pl.ds(0, half)], sent.at[S_W])
    finish(u)
    each(left, u, own_rows, fin, f_s)
    each(left, u, second & own_cross, fcr, h_s)


def by_kernel(n, mlp_inputs, enc_weight, enc_bias, dec_weight, dec_cross, dec_bias):
    x, enc, dec, cross = mlp_inputs[0], enc_weight[0], dec_weight[0].T, dec_cross.T
    r = x.shape[0] // n
    k, width = enc.shape
    columns, half = dec.shape[0], cross.shape[0]
    pieces = r // UNIT
    steps, rows = pieces * n, n * UNIT
    subs = len(parts_of(steps)[0])
    vmem = pl.BlockSpec(memory_space=pltpu.VMEM)
    hbm = pl.BlockSpec(memory_space=pl.ANY)
    dma = pltpu.SemaphoreType.DMA
    scratch = [
        pltpu.VMEM((r, x.shape[1]), BF16),
        pltpu.VMEM(enc.shape, BF16),
        pltpu.VMEM(dec.shape, BF16),
        pltpu.VMEM((2 * half, width), BF16),
        pltpu.VMEM((pieces, n, UNIT, k), BF16),
        pltpu.VMEM((pieces, n, rows, k), BF16),
        pltpu.VMEM((steps, rows, width), F32),
        pltpu.VMEM((steps, rows, width), BF16),
        pltpu.VMEM((steps, rows, width), BF16),
        pltpu.VMEM((max(DIRECT_IN, 1), rows // 2, width), BF16),
        pltpu.VMEM((steps, rows // 2, width), BF16),
        pltpu.VMEM((steps, rows // 2, width), BF16),
        pltpu.VMEM((steps, rows, width), BF16),
        pltpu.VMEM((pieces, rows, columns), F32),
        pltpu.VMEM((steps, rows, columns), BF16),
        pltpu.VMEM((steps, rows, columns), BF16),
        pltpu.VMEM((steps, rows, 2 * half), BF16),
        pltpu.VMEM((steps, rows, 2 * half), BF16),
        pltpu.VMEM((pieces, rows, columns), BF16),
        pltpu.VMEM((pieces, 2, rows, half), BF16),
        pltpu.VMEM((pieces, n, UNIT, columns), BF16),
        pltpu.VMEM((pieces, 2 * n, UNIT, half), BF16),
        dma((4,)), dma((1,)), dma((pieces, 2)), dma((pieces, n, 2)),
        dma((subs, 2)), dma((2 * max(DIRECT_IN, 1),)), dma((subs,)), dma((subs,)),
        dma((pieces,)), dma((pieces,)), dma((pieces,)), dma((pieces,)),
        dma((pieces,)), dma((pieces,)), dma((pieces,)), dma((pieces,)), dma((7,)),
    ]
    out = pl.pallas_call(
        functools.partial(kernel, n),
        out_shape=jax.ShapeDtypeStruct((x.shape[0], columns), BF16),
        in_specs=[hbm, hbm, vmem, hbm, hbm, vmem],
        out_specs=vmem,
        scratch_shapes=scratch,
        compiler_params=pltpu.CompilerParams(
            collective_id=0, has_side_effects=True, vmem_limit_bytes=56 * 2**20
        ),
    )(x, enc, enc_bias, dec, cross, dec_bias)
    return out[None]


def solution(mesh):
    placed = (
        P("layer", "seq", None),
        P("layer", "seq", "feat"),
        P("layer", "feat"),
        P("layer", "feat", "seq"),
        P("feat", ("layer", "seq")),
        P("layer", "feat"),
    )
    groups = mesh.shape["feat"]

    def body(mlp_inputs, *rest):
        fits = groups == LINE and mesh.shape["seq"] == LINE and mlp_inputs.shape[1] % (UNIT * groups) == 0
        if fits and mesh.shape["layer"] == 2 and rest[0].shape[2] % 256 == 0:
            return by_kernel(groups, mlp_inputs, *rest)
        return per_device(mlp_inputs, *rest)

    return jax.shard_map(
        body, mesh=mesh, in_specs=placed, out_specs=P("layer", "seq", "feat"), check_vma=False
    )
```

```python
import functools

import jax
import jax.numpy as jnp
from jax import lax
from jax.experimental import pallas as pl
from jax.experimental.pallas import tpu as pltpu
from jax.sharding import PartitionSpec as P

MESH = pl.DeviceIdType.MESH
F32, BF16 = jnp.float32, jnp.bfloat16


def passed_along(x, axis, by):
    devices = lax.axis_size(axis)
    pairs = [(i, i + by) for i in range(devices) if 0 <= i + by < devices]
    return lax.ppermute(x, axis, pairs)


def per_device(mlp_inputs, enc_weight, enc_bias, dec_weight, dec_cross, dec_bias):
    token_rows = mlp_inputs[0]
    layer_index = lax.axis_index("layer")
    pre_acts = jnp.dot(
        token_rows,
        lax.all_gather(enc_weight[0], "seq", axis=0, tiled=True),
        preferred_element_type=F32,
    )
    features = jnp.maximum(pre_acts + enc_bias[0], 0.0).astype(BF16)
    own_terms = jnp.dot(
        features,
        lax.all_gather(dec_weight[0], "seq", axis=1, tiled=True),
        preferred_element_type=F32,
    )
    half_rows = features.shape[0] // 2
    sent_half = passed_along(features[half_rows:], "layer", 1)
    cross_input = jnp.where(layer_index == 0, features[:half_rows], sent_half)
    cross_terms = jnp.dot(
        cross_input,
        lax.all_gather(dec_cross, ("layer", "seq"), axis=1, tiled=True),
        preferred_element_type=F32,
    )
    own_sums, cross_sums = (
        lax.psum_scatter(own_terms, "feat", scatter_dimension=1, tiled=True),
        lax.psum_scatter(cross_terms, "feat", scatter_dimension=1, tiled=True),
    )
    moved_sums = passed_along(cross_sums, "layer", 1)
    cross_full = jnp.concatenate([moved_sums, cross_sums], axis=0)
    total = own_sums + dec_bias[0] + jnp.where(layer_index == 1, cross_full, 0.0)
    return total.astype(BF16)[None]


UNIT = 16
LINE = 4
FINE_IN, FINE_OUT = 2, 2
DIRECT_IN, DIRECT_OUT = 0, 0
STEP_LAGS = {
    "own": 1.1, "forward": 2.2, "decode": 4.0, "sum": 3.5, "encode": -2.1, "edge_encode": -5.0,
}
FIRST_PIECE = ((0.01, 0.2), (0.1, 0.3), (0.6, 0.7))
SPREAD = 0.5


def decoded(features, columns):
    return lax.dot_general(features, columns, (((1,), (1,)), ((), ())), preferred_element_type=F32)


def cuts_of(s, steps):
    return 2 if s < FINE_IN or s >= steps - FINE_OUT else 1


def parts_of(steps):
    parts, start = [], []
    for s in range(steps):
        start.append(len(parts))
        parts += [(s, c, cuts_of(s, steps)) for c in range(cuts_of(s, steps))]
    return parts, start


def kernel(
    n, x_hbm, enc_hbm, encb_ref, dec_hbm, cross_hbm, decb_ref, out_ref,
    xv, enc_ref, dec_ref, cross_ref, xsend, xall, pf, psend, prec, drec, qsend, qrec, feats,
    oown, osend, orecv, csend, crecv, rsum, crs, fin, fcr,
    ld_sem, cw_r, x1_r, x2_r, p_r, d_r, q_r, g_r, o_r, c_r, f_r, h_r,
    x1_s, x2_s, f_s, h_s, sent,
):
    layer, f, z = lax.axis_index("layer"), lax.axis_index("feat"), lax.axis_index("seq")
    k = enc_ref.shape[0]
    half = cross_hbm.shape[0]
    r, width = xv.shape[0], enc_ref.shape[1]
    pieces = r // UNIT
    steps = pieces * n
    parts, start = parts_of(steps)
    mid = n // 2
    hrows = mid * UNIT
    first, second = layer == 0, layer == 1
    side = lax.div(z, mid)
    inner = (z == mid - 1) | (z == mid)
    edge = (z == 0) | (z == n - 1)
    z_edge, z_inner, z_other, z_far = side * (n - 1), mid - 1 + side, mid - side, (1 - side) * (n - 1)
    far = pl.ds(pl.multiple_of(side * hrows, hrows), hrows)
    near = pl.ds(pl.multiple_of((1 - side) * hrows, hrows), hrows)

    def peer(dx):
        total, bit = 0, 1
        while bit < n:
            own = lax.rem(lax.div(f, bit), 2)
            total = total + bit * ((1 - own) if dx & bit else own)
            bit *= 2
        return total

    sequence = [(0, dx) for dx in range(n)]
    sequence += [(u, dx) for u in range(1, pieces) for dx in range(n - 1, 0, -1)]
    sequence += [(u, 0) for u in range(1, pieces)]

    def split(s):
        return sequence[s]

    def outgoing(u, dx):
        return u * (n - 1) + dx - 1

    def cols(i):
        _, c, cuts = parts[i]
        return pl.ds(c * (width // cuts), width // cuts)

    def block(t):
        return pl.ds(pl.multiple_of(t * UNIT, UNIT), UNIT)

    def copy(src, dst, ss, rs, to):
        a, b, c = to
        return pltpu.make_async_remote_copy(
            src_ref=src, dst_ref=dst, send_sem=ss, recv_sem=rs,
            device_id={"layer": a, "feat": b, "seq": c}, device_id_type=MESH,
        )

    role = [None]

    def on(cond, run):
        if cond is None or (role[0] is not None and cond is role[0]):
            run()
        elif role[0] is not None and (cond is edge or cond is inner):
            return
        else:
            pl.when(cond)(run)

    def send(cond, make):
        on(cond, lambda: make().start())

    def arrive(cond, dst, sem):
        on(cond, lambda: copy(dst, dst, sem, sem, (layer, f, z)).wait_recv())

    def left(cond, src, sem):
        on(cond, lambda: copy(src, src, sem, sem, (layer, f, z)).wait_send())

    turns = [lax.rem(z + d, n) for d in (mid, mid + 1, mid - 1, 0)]
    S_P, S_Q, S_G, S_E, S_O, S_C, S_W = range(7)

    loads = [
        pltpu.make_async_copy(x_hbm.at[pl.ds(pl.multiple_of(f * r, UNIT), r)], xv, ld_sem.at[0]),
        pltpu.make_async_copy(enc_hbm, enc_ref, ld_sem.at[1]),
        pltpu.make_async_copy(cross_hbm, cross_ref.at[pl.ds(0, half)], ld_sem.at[2]),
        pltpu.make_async_copy(dec_hbm, dec_ref, ld_sem.at[3]),
    ]
    for load in loads:
        load.start()

    barrier = pltpu.get_barrier_semaphore()
    greeted = []
    for a in range(n):
        for b in range(n):
            if a or b:
                greeted.append((layer, lax.rem(f + a, n), lax.rem(z + b, n)))
    greeted += [(1 - layer, lax.rem(f + a, n), z) for a in range(n)]
    for a, b, c in greeted:
        pl.semaphore_signal(
            barrier, inc=1, device_id={"layer": a, "feat": b, "seq": c}, device_id_type=MESH
        )

    loads[0].wait()
    for u in range(pieces):
        for t in range(n):
            xsend[u, t] = xv[u * UNIT:(u + 1) * UNIT, t * k:(t + 1) * k]
        if u == 0:
            pl.semaphore_wait(barrier, len(greeted))
        for d in range(n - 1, 0, -1):
            for sign in (1, -1):
                t = z + sign * d
                send((t < n) & (t >= 0), lambda t=t, u=u: copy(
                    xsend.at[u, t], xall.at[u, f, block(z)], x1_s.at[u], x1_r.at[u, lax.rem(side + lax.div(t, mid), 2)], (layer, f, t)))
        xall[u, f, block(z), :] = xsend[u, z]
    loads[2].wait()
    send(second, lambda: copy(
        cross_ref.at[pl.ds(0, half)], cross_ref.at[pl.ds(half, half)], sent.at[S_W], cw_r.at[0], (0, f, z)))

    halves = ((far, 0), (near, 1))

    def spread(u, half):
        part, h = half
        arrive(None, xall.at[u, f, pl.ds(0, (mid - 1 + h) * UNIT)], x1_r.at[u, h])
        for dx in range(1, n):
            send(None, lambda dx=dx: copy(
                xall.at[u, f, part], xall.at[u, f, part], x2_s.at[u], x2_r.at[u, dx, h], (layer, peer(dx), z)))

    def encode(s, chosen):
        u, dx = split(s)
        p = peer(dx)
        if dx:
            for part, h in chosen:
                arrive(None, xall.at[u, p, part], x2_r.at[u, dx, h])
        rows = chosen[0][0] if len(chosen) == 1 else pl.ds(0, 2 * hrows)
        pf[s, rows] = jnp.dot(xall[u, p, rows], enc_ref[...], preferred_element_type=F32)

        def rounded():
            psend[s, rows] = pf[s, rows].astype(BF16)
        on(edge, rounded)
        for i in range(start[s], start[s] + cuts_of(s, steps)):
            for part, h in chosen:
                at = lambda i=i, part=part: psend.at[s, part, cols(i)]
                if h == 0 and s < DIRECT_IN:
                    send(edge, lambda i=i, at=at: copy(
                        at(), drec.at[s, :, cols(i)], sent.at[S_P], d_r.at[i], (layer, f, z_other)))
                else:
                    send(edge, lambda i=i, at=at, part=part, h=h: copy(
                        at(), prec.at[s, part, cols(i)], sent.at[S_P], p_r.at[i, h], (layer, f, z_inner)))

    def relay(i):
        s = parts[i][0]
        if s >= DIRECT_IN:
            arrive(inner, prec.at[s, far, cols(i)], p_r.at[i, 0])

        def passed():
            total = pf[s, far, cols(i)]
            if s >= DIRECT_IN:
                total += prec[s, far, cols(i)].astype(F32)
            qsend[s, :, cols(i)] = total.astype(BF16)
        on(inner, passed)
        send(inner, lambda: copy(
            qsend.at[s, :, cols(i)], qrec.at[s, :, cols(i)], sent.at[S_Q], q_r.at[i], (layer, f, z_other)))

    def own(i):
        s = parts[i][0]
        arrive(inner, prec.at[s, near, cols(i)], p_r.at[i, 1])
        if s < DIRECT_IN:
            arrive(inner, drec.at[s, :, cols(i)], d_r.at[i])
        arrive(inner, qrec.at[s, :, cols(i)], q_r.at[i])

        def activated():
            total = pf[s, near, cols(i)] + encb_ref[:, cols(i)]
            total += prec[s, near, cols(i)].astype(F32)
            total += qrec[s, :, cols(i)].astype(F32)
            if s < DIRECT_IN:
                total += drec[s, :, cols(i)].astype(F32)
            feats[s, near, cols(i)] = jnp.maximum(total, 0.0).astype(BF16)
        on(inner, activated)
        at = lambda: feats.at[s, near, cols(i)]
        to = [(g_r.at[i], S_G, z_other), (p_r.at[start[s], 0], S_E, z_edge)]
        if s >= steps - DIRECT_OUT:
            to = [(p_r.at[start[s], 0], S_E, z_far)] + to
        for sem, ss, zz in to:
            send(inner, lambda sem=sem, ss=ss, zz=zz: copy(at(), at(), sent.at[ss], sem, (layer, f, zz)))

    def forward(i):
        s = parts[i][0]
        at = lambda: feats.at[s, far, cols(i)]
        arrive(inner, at(), g_r.at[i])
        if s < steps - DIRECT_OUT:
            send(inner, lambda: copy(at(), at(), sent.at[S_E], p_r.at[start[s], 0], (layer, f, z_edge)))

    def decode(s):
        u, dx = split(s)
        arrive(edge, feats.at[s], p_r.at[start[s], 0])

        def crossed():
            @pl.when(first)
            def _():
                csend[u * n + dx] = decoded(feats[s], cross_ref[...]).astype(BF16)
            send(first, lambda: copy(
                csend.at[u * n + dx], crecv.at[u * n + dx], sent.at[S_C], c_r.at[u], (1, peer(dx), z)))

        if not dx:
            crossed()
        terms = decoded(feats[s], dec_ref[...])
        if dx:
            osend[outgoing(u, dx)] = terms.astype(BF16)
            send(None, lambda: copy(
                osend.at[outgoing(u, dx)], orecv.at[outgoing(u, dx)], sent.at[S_O], o_r.at[u], (layer, peer(dx), z)))
            crossed()
        else:
            oown[u] = terms

    def summed(u):
        arrive(None, orecv.at[pl.ds(u * (n - 1), n - 1)], o_r.at[u])
        total = oown[u]
        for dx in range(1, n):
            total += orecv[outgoing(u, dx)].astype(F32)
        rsum[u] = total.astype(BF16)
        for t in turns:
            here = (z == t) & (f == z)
            send(jnp.logical_not(here), lambda t=t: copy(
                rsum.at[u, block(t)], fin.at[u, f], f_s.at[u], f_r.at[u], (layer, z, t)))

        @pl.when(f == z)
        def _():
            fin[u, f] = rsum[u, block(z), :]

    def crossed_sum(u):
        arrive(second, crecv.at[pl.ds(u * n, n)], c_r.at[u])

        @pl.when(second)
        def _():
            sums = crecv[u * n].astype(F32)
            for i in range(1, n):
                sums += crecv[u * n + i].astype(F32)
            for h in range(2):
                crs[u, h] = sums[:, h * half:(h + 1) * half].astype(BF16)
        slot = lax.rem(z, 2) * n + f
        for h in range(2):
            to = h * mid + lax.div(z, 2)
            for t in turns:
                here = (z == t) & (f == to)
                send(second & jnp.logical_not(here), lambda h=h, t=t, to=to: copy(
                    crs.at[u, h, block(t)], fcr.at[u, slot],
                    h_s.at[u], h_r.at[u], (layer, to, t)))

            @pl.when(second & (f == to))
            def _(h=h):
                fcr[u, slot] = crs[u, h, block(z), :]

    own_rows = f == z
    own_cross = lax.rem(f, 2) == lax.div(z, 2)

    def each(run, u, mine, whole, other):
        count = whole.shape[1]
        run(mine, whole.at[u, pl.ds(0, count - 1)], other.at[u])
        rest = jnp.logical_not(mine) if mine is own_rows else second & jnp.logical_not(own_cross)
        run(rest, whole.at[u], other.at[u])

    def finish(u):
        each(arrive, u, own_rows, fin, f_r)
        each(arrive, u, second & own_cross, fcr, h_r)
        for g in range(n):
            part = slice(g * r + u * UNIT, g * r + (u + 1) * UNIT)

            @pl.when(first)
            def _():
                out_ref[part] = (fin[u, g].astype(F32) + decb_ref[...]).astype(BF16)

            @pl.when(second)
            def _():
                cross = jnp.concatenate([fcr[u, g].astype(F32), fcr[u, n + g].astype(F32)], axis=1)
                out_ref[part] = (fin[u, g].astype(F32) + cross + decb_ref[...]).astype(BF16)

    for h in range(2):
        spread(0, halves[h])
        if h == 0:
            loads[1].wait()
        encode(0, halves[h:h + 1])

    last = [max(s for s in range(steps) if split(s)[0] == u) for u in range(pieces)]

    def ordered(cond):
        events = []

        def place(time, rank, run, *given):
            events.append((time, rank, len(events), run, given))

        if cond is inner:
            for i, (s, c, cuts) in enumerate(parts):
                begin = s + c / cuts
                place(begin, 0, relay, i)
                place(begin + STEP_LAGS["own"], 1, own, i)
                place(begin + STEP_LAGS["forward"], 2, forward, i)
        for dx in range(1, n):
            for h in range(2):
                place(FIRST_PIECE[dx - 1][h], 3, encode, dx, halves[h:h + 1])
        for u in range(1, pieces):
            for h in range(2):
                place(SPREAD * u, 3, spread, u, halves[h])
        decoded_at = []
        for s in range(steps):
            if s >= n:
                early = s + STEP_LAGS["encode"] if cond is inner else s + STEP_LAGS["edge_encode"]
                place(max(early, 1.05 + 0.3 * (s - n)), 3, encode, s, halves)
            time = s + STEP_LAGS["decode"]
            decoded_at.append(time)
            place(time, 4, decode, s)
        for u in range(pieces):
            late = decoded_at[last[u]] + (0 if u else STEP_LAGS["sum"])
            place(late, 5, summed, u)
            place(late if u == 0 else decoded_at[-1], 6, crossed_sum, u)
        place(steps - 2.5 + STEP_LAGS["decode"], 5, finish, 0)
        place(0.5, 6, loads[3].wait)
        place(0.5, 7, lambda: arrive(first, cross_ref.at[pl.ds(half, half)], cw_r.at[0]))
        return sorted(events, key=lambda e: e[:3])

    for cond in (edge, inner):
        @pl.when(cond)
        def _(cond=cond):
            role[0] = cond
            for _, _, _, run, given in ordered(cond):
                run(*given)
            role[0] = None
    for u in range(pieces - 1):
        if u:
            finish(u)
        left(None, xall.at[u, f, pl.ds(0, (n - 1) * UNIT)], x1_s.at[u])
        left(None, xall.at[u, pl.ds(0, n - 1)], x2_s.at[u])
        each(left, u, own_rows, fin, f_s)
        each(left, u, second & own_cross, fcr, h_s)
    u = pieces - 1
    left(None, xall.at[u, f, pl.ds(0, (n - 1) * UNIT)], x1_s.at[u])
    left(None, xall.at[u, pl.ds(0, n - 1)], x2_s.at[u])
    left(edge, psend, sent.at[S_P])
    left(inner, qsend, sent.at[S_Q])
    left(inner, qsend, sent.at[S_G])
    left(inner, feats, sent.at[S_E])
    left(None, osend.at[pl.ds(0, steps - pieces)], sent.at[S_O])
    left(first, csend, sent.at[S_C])
    left(second, cross_ref.at[pl.ds(0, half)], sent.at[S_W])
    finish(u)
    each(left, u, own_rows, fin, f_s)
    each(left, u, second & own_cross, fcr, h_s)


def by_kernel(n, mlp_inputs, enc_weight, enc_bias, dec_weight, dec_cross, dec_bias):
    x, enc, dec, cross = mlp_inputs[0], enc_weight[0], dec_weight[0].T, dec_cross.T
    r = x.shape[0] // n
    k, width = enc.shape
    columns, half = dec.shape[0], cross.shape[0]
    pieces = r // UNIT
    steps, rows = pieces * n, n * UNIT
    subs = len(parts_of(steps)[0])
    vmem = pl.BlockSpec(memory_space=pltpu.VMEM)
    hbm = pl.BlockSpec(memory_space=pl.ANY)
    dma = pltpu.SemaphoreType.DMA
    scratch = [
        pltpu.VMEM((r, x.shape[1]), BF16),
        pltpu.VMEM(enc.shape, BF16),
        pltpu.VMEM(dec.shape, BF16),
        pltpu.VMEM((2 * half, width), BF16),
        pltpu.VMEM((pieces, n, UNIT, k), BF16),
        pltpu.VMEM((pieces, n, rows, k), BF16),
        pltpu.VMEM((steps, rows, width), F32),
        pltpu.VMEM((steps, rows, width), BF16),
        pltpu.VMEM((steps, rows, width), BF16),
        pltpu.VMEM((max(DIRECT_IN, 1), rows // 2, width), BF16),
        pltpu.VMEM((steps, rows // 2, width), BF16),
        pltpu.VMEM((steps, rows // 2, width), BF16),
        pltpu.VMEM((steps, rows, width), BF16),
        pltpu.VMEM((pieces, rows, columns), F32),
        pltpu.VMEM((steps, rows, columns), BF16),
        pltpu.VMEM((steps, rows, columns), BF16),
        pltpu.VMEM((steps, rows, 2 * half), BF16),
        pltpu.VMEM((steps, rows, 2 * half), BF16),
        pltpu.VMEM((pieces, rows, columns), BF16),
        pltpu.VMEM((pieces, 2, rows, half), BF16),
        pltpu.VMEM((pieces, n, UNIT, columns), BF16),
        pltpu.VMEM((pieces, 2 * n, UNIT, half), BF16),
        dma((4,)), dma((1,)), dma((pieces, 2)), dma((pieces, n, 2)),
        dma((subs, 2)), dma((2 * max(DIRECT_IN, 1),)), dma((subs,)), dma((subs,)),
        dma((pieces,)), dma((pieces,)), dma((pieces,)), dma((pieces,)),
        dma((pieces,)), dma((pieces,)), dma((pieces,)), dma((pieces,)), dma((7,)),
    ]
    out = pl.pallas_call(
        functools.partial(kernel, n),
        out_shape=jax.ShapeDtypeStruct((x.shape[0], columns), BF16),
        in_specs=[hbm, hbm, vmem, hbm, hbm, vmem],
        out_specs=vmem,
        scratch_shapes=scratch,
        compiler_params=pltpu.CompilerParams(
            collective_id=0, has_side_effects=True, vmem_limit_bytes=56 * 2**20
        ),
    )(x, enc, enc_bias, dec, cross, dec_bias)
    return out[None]


def solution(mesh):
    placed = (
        P("layer", "seq", None),
        P("layer", "seq", "feat"),
        P("layer", "feat"),
        P("layer", "feat", "seq"),
        P("feat", ("layer", "seq")),
        P("layer", "feat"),
    )
    groups = mesh.shape["feat"]

    def body(mlp_inputs, *rest):
        fits = groups == LINE and mesh.shape["seq"] == LINE and mlp_inputs.shape[1] % (UNIT * groups) == 0
        if fits and mesh.shape["layer"] == 2 and rest[0].shape[2] % 256 == 0:
            return by_kernel(groups, mlp_inputs, *rest)
        return per_device(mlp_inputs, *rest)

    return jax.shard_map(
        body, mesh=mesh, in_specs=placed, out_specs=P("layer", "seq", "feat"), check_vma=False
    )
```

```python
import functools

import jax
import jax.numpy as jnp
from jax import lax
from jax.experimental import pallas as pl
from jax.experimental.pallas import tpu as pltpu
from jax.sharding import PartitionSpec as P

MESH = pl.DeviceIdType.MESH
F32, BF16 = jnp.float32, jnp.bfloat16


def passed_along(x, axis, by):
    devices = lax.axis_size(axis)
    pairs = [(i, i + by) for i in range(devices) if 0 <= i + by < devices]
    return lax.ppermute(x, axis, pairs)


def per_device(mlp_inputs, enc_weight, enc_bias, dec_weight, dec_cross, dec_bias):
    token_rows = mlp_inputs[0]
    layer_index = lax.axis_index("layer")
    pre_acts = jnp.dot(
        token_rows,
        lax.all_gather(enc_weight[0], "seq", axis=0, tiled=True),
        preferred_element_type=F32,
    )
    features = jnp.maximum(pre_acts + enc_bias[0], 0.0).astype(BF16)
    own_terms = jnp.dot(
        features,
        lax.all_gather(dec_weight[0], "seq", axis=1, tiled=True),
        preferred_element_type=F32,
    )
    half_rows = features.shape[0] // 2
    sent_half = passed_along(features[half_rows:], "layer", 1)
    cross_input = jnp.where(layer_index == 0, features[:half_rows], sent_half)
    cross_terms = jnp.dot(
        cross_input,
        lax.all_gather(dec_cross, ("layer", "seq"), axis=1, tiled=True),
        preferred_element_type=F32,
    )
    own_sums, cross_sums = (
        lax.psum_scatter(own_terms, "feat", scatter_dimension=1, tiled=True),
        lax.psum_scatter(cross_terms, "feat", scatter_dimension=1, tiled=True),
    )
    moved_sums = passed_along(cross_sums, "layer", 1)
    cross_full = jnp.concatenate([moved_sums, cross_sums], axis=0)
    total = own_sums + dec_bias[0] + jnp.where(layer_index == 1, cross_full, 0.0)
    return total.astype(BF16)[None]


UNIT = 16
LINE = 4
FINE_IN, FINE_OUT = 2, 2
DIRECT_IN, DIRECT_OUT = 0, 0
STEP_LAGS = {
    "own": 1.1, "forward": 2.2, "decode": 4.0, "sum": 3.5, "encode": -2.1, "edge_encode": -5.0,
}
FIRST_PIECE = ((0.01, 0.2), (0.1, 0.3), (0.6, 0.7))
SPREAD = 0.5


def decoded(features, columns):
    return lax.dot_general(features, columns, (((1,), (1,)), ((), ())), preferred_element_type=F32)


def cuts_of(s, steps):
    return 2 if s < FINE_IN or s >= steps - FINE_OUT else 1


def parts_of(steps):
    parts, start = [], []
    for s in range(steps):
        start.append(len(parts))
        parts += [(s, c, cuts_of(s, steps)) for c in range(cuts_of(s, steps))]
    return parts, start


def kernel(
    n, x_hbm, enc_hbm, encb_ref, dec_hbm, cross_hbm, decb_ref, out_ref,
    xv, enc_ref, dec_ref, cross_ref, xsend, xall, pf, psend, prec, drec, qsend, qrec, feats,
    oown, osend, orecv, csend, crecv, rsum, crs, fin, fcr,
    ld_sem, cw_r, x1_r, x2_r, p_r, d_r, q_r, g_r, o_r, c_r, f_r, h_r,
    x1_s, x2_s, f_s, h_s, sent,
):
    layer, f, z = lax.axis_index("layer"), lax.axis_index("feat"), lax.axis_index("seq")
    k = enc_ref.shape[0]
    half = cross_hbm.shape[0]
    r, width = xv.shape[0], enc_ref.shape[1]
    pieces = r // UNIT
    steps = pieces * n
    parts, start = parts_of(steps)
    mid = n // 2
    hrows = mid * UNIT
    first, second = layer == 0, layer == 1
    side = lax.div(z, mid)
    inner = (z == mid - 1) | (z == mid)
    edge = (z == 0) | (z == n - 1)
    z_edge, z_inner, z_other, z_far = side * (n - 1), mid - 1 + side, mid - side, (1 - side) * (n - 1)
    far = pl.ds(pl.multiple_of(side * hrows, hrows), hrows)
    near = pl.ds(pl.multiple_of((1 - side) * hrows, hrows), hrows)

    def peer(dx):
        total, bit = 0, 1
        while bit < n:
            own = lax.rem(lax.div(f, bit), 2)
            total = total + bit * ((1 - own) if dx & bit else own)
            bit *= 2
        return total

    sequence = [(0, dx) for dx in range(n)]
    sequence += [(u, dx) for u in range(1, pieces) for dx in range(n - 1, 0, -1)]
    sequence += [(u, 0) for u in range(1, pieces)]

    def split(s):
        return sequence[s]

    def outgoing(u, dx):
        return u * (n - 1) + dx - 1

    def cols(i):
        _, c, cuts = parts[i]
        return pl.ds(c * (width // cuts), width // cuts)

    def block(t):
        return pl.ds(pl.multiple_of(t * UNIT, UNIT), UNIT)

    def copy(src, dst, ss, rs, to):
        a, b, c = to
        return pltpu.make_async_remote_copy(
            src_ref=src, dst_ref=dst, send_sem=ss, recv_sem=rs,
            device_id={"layer": a, "feat": b, "seq": c}, device_id_type=MESH,
        )

    role = [None]

    def on(cond, run):
        if cond is None or (role[0] is not None and cond is role[0]):
            run()
        elif role[0] is not None and (cond is edge or cond is inner):
            return
        else:
            pl.when(cond)(run)

    def send(cond, make):
        on(cond, lambda: make().start())

    def arrive(cond, dst, sem):
        on(cond, lambda: copy(dst, dst, sem, sem, (layer, f, z)).wait_recv())

    def left(cond, src, sem):
        on(cond, lambda: copy(src, src, sem, sem, (layer, f, z)).wait_send())

    turns = [lax.rem(z + d, n) for d in (mid, mid + 1, mid - 1, 0)]
    S_P, S_Q, S_G, S_E, S_O, S_C, S_W = range(7)

    loads = [
        pltpu.make_async_copy(x_hbm.at[pl.ds(pl.multiple_of(f * r, UNIT), r)], xv, ld_sem.at[0]),
        pltpu.make_async_copy(enc_hbm, enc_ref, ld_sem.at[1]),
        pltpu.make_async_copy(cross_hbm, cross_ref.at[pl.ds(0, half)], ld_sem.at[2]),
        pltpu.make_async_copy(dec_hbm, dec_ref, ld_sem.at[3]),
    ]
    for load in loads:
        load.start()

    barrier = pltpu.get_barrier_semaphore()
    greeted = [(layer, f, lax.rem(z + a, n)) for a in range(1, n)]
    greeted += [(layer, lax.rem(f + a, n), z) for a in range(1, n)]
    greeted += [(1 - layer, lax.rem(f + a, n), z) for a in range(n)]
    for a, b, c in greeted:
        pl.semaphore_signal(
            barrier, inc=1, device_id={"layer": a, "feat": b, "seq": c}, device_id_type=MESH
        )

    loads[0].wait()
    for u in range(pieces):
        for t in range(n):
            xsend[u, t] = xv[u * UNIT:(u + 1) * UNIT, t * k:(t + 1) * k]
        if u == 0:
            pl.semaphore_wait(barrier, len(greeted))
        for d in range(n - 1, 0, -1):
            for sign in (1, -1):
                t = z + sign * d
                send((t < n) & (t >= 0), lambda t=t, u=u: copy(
                    xsend.at[u, t], xall.at[u, f, block(z)], x1_s.at[u], x1_r.at[u, lax.rem(side + lax.div(t, mid), 2)], (layer, f, t)))
        xall[u, f, block(z), :] = xsend[u, z]
    loads[2].wait()
    send(second, lambda: copy(
        cross_ref.at[pl.ds(0, half)], cross_ref.at[pl.ds(half, half)], sent.at[S_W], cw_r.at[0], (0, f, z)))

    halves = ((far, 0), (near, 1))

    def spread(u, half):
        part, h = half
        arrive(None, xall.at[u, f, pl.ds(0, (mid - 1 + h) * UNIT)], x1_r.at[u, h])
        for dx in range(1, n):
            send(None, lambda dx=dx: copy(
                xall.at[u, f, part], xall.at[u, f, part], x2_s.at[u], x2_r.at[u, dx, h], (layer, peer(dx), z)))

    def encode(s, chosen):
        u, dx = split(s)
        p = peer(dx)
        if dx:
            for part, h in chosen:
                arrive(None, xall.at[u, p, part], x2_r.at[u, dx, h])
        rows = chosen[0][0] if len(chosen) == 1 else pl.ds(0, 2 * hrows)
        pf[s, rows] = jnp.dot(xall[u, p, rows], enc_ref[...], preferred_element_type=F32)

        def rounded():
            psend[s, rows] = pf[s, rows].astype(BF16)
        on(edge, rounded)
        for i in range(start[s], start[s] + cuts_of(s, steps)):
            for part, h in chosen:
                at = lambda i=i, part=part: psend.at[s, part, cols(i)]
                if h == 0 and s < DIRECT_IN:
                    send(edge, lambda i=i, at=at: copy(
                        at(), drec.at[s, :, cols(i)], sent.at[S_P], d_r.at[i], (layer, f, z_other)))
                else:
                    send(edge, lambda i=i, at=at, part=part, h=h: copy(
                        at(), prec.at[s, part, cols(i)], sent.at[S_P], p_r.at[i, h], (layer, f, z_inner)))

    def relay(i):
        s = parts[i][0]
        if s >= DIRECT_IN:
            arrive(inner, prec.at[s, far, cols(i)], p_r.at[i, 0])

        def passed():
            total = pf[s, far, cols(i)]
            if s >= DIRECT_IN:
                total += prec[s, far, cols(i)].astype(F32)
            qsend[s, :, cols(i)] = total.astype(BF16)
        on(inner, passed)
        send(inner, lambda: copy(
            qsend.at[s, :, cols(i)], qrec.at[s, :, cols(i)], sent.at[S_Q], q_r.at[i], (layer, f, z_other)))

    def own(i):
        s = parts[i][0]
        arrive(inner, prec.at[s, near, cols(i)], p_r.at[i, 1])
        if s < DIRECT_IN:
            arrive(inner, drec.at[s, :, cols(i)], d_r.at[i])
        arrive(inner, qrec.at[s, :, cols(i)], q_r.at[i])

        def activated():
            total = pf[s, near, cols(i)] + encb_ref[:, cols(i)]
            total += prec[s, near, cols(i)].astype(F32)
            total += qrec[s, :, cols(i)].astype(F32)
            if s < DIRECT_IN:
                total += drec[s, :, cols(i)].astype(F32)
            feats[s, near, cols(i)] = jnp.maximum(total, 0.0).astype(BF16)
        on(inner, activated)
        at = lambda: feats.at[s, near, cols(i)]
        to = [(g_r.at[i], S_G, z_other), (p_r.at[start[s], 0], S_E, z_edge)]
        if s >= steps - DIRECT_OUT:
            to = [(p_r.at[start[s], 0], S_E, z_far)] + to
        for sem, ss, zz in to:
            send(inner, lambda sem=sem, ss=ss, zz=zz: copy(at(), at(), sent.at[ss], sem, (layer, f, zz)))

    def forward(i):
        s = parts[i][0]
        at = lambda: feats.at[s, far, cols(i)]
        arrive(inner, at(), g_r.at[i])
        if s < steps - DIRECT_OUT:
            send(inner, lambda: copy(at(), at(), sent.at[S_E], p_r.at[start[s], 0], (layer, f, z_edge)))

    def decode(s):
        u, dx = split(s)
        arrive(edge, feats.at[s], p_r.at[start[s], 0])

        def crossed():
            @pl.when(first)
            def _():
                csend[u * n + dx] = decoded(feats[s], cross_ref[...]).astype(BF16)
            send(first, lambda: copy(
                csend.at[u * n + dx], crecv.at[u * n + dx], sent.at[S_C], c_r.at[u], (1, peer(dx), z)))

        if not dx:
            crossed()
        terms = decoded(feats[s], dec_ref[...])
        if dx:
            osend[outgoing(u, dx)] = terms.astype(BF16)
            send(None, lambda: copy(
                osend.at[outgoing(u, dx)], orecv.at[outgoing(u, dx)], sent.at[S_O], o_r.at[u], (layer, peer(dx), z)))
            crossed()
        else:
            oown[u] = terms

    def summed(u):
        arrive(None, orecv.at[pl.ds(u * (n - 1), n - 1)], o_r.at[u])
        total = oown[u]
        for dx in range(1, n):
            total += orecv[outgoing(u, dx)].astype(F32)
        rsum[u] = total.astype(BF16)
        for t in turns:
            here = (z == t) & (f == z)
            send(jnp.logical_not(here), lambda t=t: copy(
                rsum.at[u, block(t)], fin.at[u, f], f_s.at[u], f_r.at[u], (layer, z, t)))

        @pl.when(f == z)
        def _():
            fin[u, f] = rsum[u, block(z), :]

    def crossed_sum(u):
        arrive(second, crecv.at[pl.ds(u * n, n)], c_r.at[u])

        @pl.when(second)
        def _():
            sums = crecv[u * n].astype(F32)
            for i in range(1, n):
                sums += crecv[u * n + i].astype(F32)
            for h in range(2):
                crs[u, h] = sums[:, h * half:(h + 1) * half].astype(BF16)
        slot = lax.rem(z, 2) * n + f
        for h in range(2):
            to = h * mid + lax.div(z, 2)
            for t in turns:
                here = (z == t) & (f == to)
                send(second & jnp.logical_not(here), lambda h=h, t=t, to=to: copy(
                    crs.at[u, h, block(t)], fcr.at[u, slot],
                    h_s.at[u], h_r.at[u], (layer, to, t)))

            @pl.when(second & (f == to))
            def _(h=h):
                fcr[u, slot] = crs[u, h, block(z), :]

    own_rows = f == z
    own_cross = lax.rem(f, 2) == lax.div(z, 2)

    def each(run, u, mine, whole, other):
        count = whole.shape[1]
        run(mine, whole.at[u, pl.ds(0, count - 1)], other.at[u])
        rest = jnp.logical_not(mine) if mine is own_rows else second & jnp.logical_not(own_cross)
        run(rest, whole.at[u], other.at[u])

    def finish(u):
        each(arrive, u, own_rows, fin, f_r)
        each(arrive, u, second & own_cross, fcr, h_r)
        for g in range(n):
            part = slice(g * r + u * UNIT, g * r + (u + 1) * UNIT)

            @pl.when(first)
            def _():
                out_ref[part] = (fin[u, g].astype(F32) + decb_ref[...]).astype(BF16)

            @pl.when(second)
            def _():
                cross = jnp.concatenate([fcr[u, g].astype(F32), fcr[u, n + g].astype(F32)], axis=1)
                out_ref[part] = (fin[u, g].astype(F32) + cross + decb_ref[...]).astype(BF16)

    for h in range(2):
        spread(0, halves[h])
        if h == 0:
            loads[1].wait()
        encode(0, halves[h:h + 1])

    last = [max(s for s in range(steps) if split(s)[0] == u) for u in range(pieces)]

    def ordered(cond):
        events = []

        def place(time, rank, run, *given):
            events.append((time, rank, len(events), run, given))

        if cond is inner:
            for i, (s, c, cuts) in enumerate(parts):
                begin = s + c / cuts
                place(begin, 0, relay, i)
                place(begin + STEP_LAGS["own"], 1, own, i)
                place(begin + STEP_LAGS["forward"], 2, forward, i)
        for dx in range(1, n):
            for h in range(2):
                place(FIRST_PIECE[dx - 1][h], 3, encode, dx, halves[h:h + 1])
        for u in range(1, pieces):
            for h in range(2):
                place(SPREAD * u, 3, spread, u, halves[h])
        decoded_at = []
        for s in range(steps):
            if s >= n:
                early = s + STEP_LAGS["encode"] if cond is inner else s + STEP_LAGS["edge_encode"]
                place(max(early, 1.05 + 0.3 * (s - n)), 3, encode, s, halves)
            time = s + STEP_LAGS["decode"]
            decoded_at.append(time)
            place(time, 4, decode, s)
        for u in range(pieces):
            late = decoded_at[last[u]] + (0 if u else STEP_LAGS["sum"])
            place(late, 5, summed, u)
            place(late if u == 0 else decoded_at[-1], 6, crossed_sum, u)
        place(steps - 2.5 + STEP_LAGS["decode"], 5, finish, 0)
        place(0.5, 6, loads[3].wait)
        place(0.5, 7, lambda: arrive(first, cross_ref.at[pl.ds(half, half)], cw_r.at[0]))
        return sorted(events, key=lambda e: e[:3])

    for cond in (edge, inner):
        @pl.when(cond)
        def _(cond=cond):
            role[0] = cond
            for _, _, _, run, given in ordered(cond):
                run(*given)
            role[0] = None
    for u in range(pieces - 1):
        if u:
            finish(u)
        left(None, xall.at[u, f, pl.ds(0, (n - 1) * UNIT)], x1_s.at[u])
        left(None, xall.at[u, pl.ds(0, n - 1)], x2_s.at[u])
        each(left, u, own_rows, fin, f_s)
        each(left, u, second & own_cross, fcr, h_s)
    u = pieces - 1
    left(None, xall.at[u, f, pl.ds(0, (n - 1) * UNIT)], x1_s.at[u])
    left(None, xall.at[u, pl.ds(0, n - 1)], x2_s.at[u])
    left(edge, psend, sent.at[S_P])
    left(inner, qsend, sent.at[S_Q])
    left(inner, qsend, sent.at[S_G])
    left(inner, feats, sent.at[S_E])
    left(None, osend.at[pl.ds(0, steps - pieces)], sent.at[S_O])
    left(first, csend, sent.at[S_C])
    left(second, cross_ref.at[pl.ds(0, half)], sent.at[S_W])
    finish(u)
    each(left, u, own_rows, fin, f_s)
    each(left, u, second & own_cross, fcr, h_s)


def by_kernel(n, mlp_inputs, enc_weight, enc_bias, dec_weight, dec_cross, dec_bias):
    x, enc, dec, cross = mlp_inputs[0], enc_weight[0], dec_weight[0].T, dec_cross.T
    r = x.shape[0] // n
    k, width = enc.shape
    columns, half = dec.shape[0], cross.shape[0]
    pieces = r // UNIT
    steps, rows = pieces * n, n * UNIT
    subs = len(parts_of(steps)[0])
    vmem = pl.BlockSpec(memory_space=pltpu.VMEM)
    hbm = pl.BlockSpec(memory_space=pl.ANY)
    dma = pltpu.SemaphoreType.DMA
    scratch = [
        pltpu.VMEM((r, x.shape[1]), BF16),
        pltpu.VMEM(enc.shape, BF16),
        pltpu.VMEM(dec.shape, BF16),
        pltpu.VMEM((2 * half, width), BF16),
        pltpu.VMEM((pieces, n, UNIT, k), BF16),
        pltpu.VMEM((pieces, n, rows, k), BF16),
        pltpu.VMEM((steps, rows, width), F32),
        pltpu.VMEM((steps, rows, width), BF16),
        pltpu.VMEM((steps, rows, width), BF16),
        pltpu.VMEM((max(DIRECT_IN, 1), rows // 2, width), BF16),
        pltpu.VMEM((steps, rows // 2, width), BF16),
        pltpu.VMEM((steps, rows // 2, width), BF16),
        pltpu.VMEM((steps, rows, width), BF16),
        pltpu.VMEM((pieces, rows, columns), F32),
        pltpu.VMEM((steps, rows, columns), BF16),
        pltpu.VMEM((steps, rows, columns), BF16),
        pltpu.VMEM((steps, rows, 2 * half), BF16),
        pltpu.VMEM((steps, rows, 2 * half), BF16),
        pltpu.VMEM((pieces, rows, columns), BF16),
        pltpu.VMEM((pieces, 2, rows, half), BF16),
        pltpu.VMEM((pieces, n, UNIT, columns), BF16),
        pltpu.VMEM((pieces, 2 * n, UNIT, half), BF16),
        dma((4,)), dma((1,)), dma((pieces, 2)), dma((pieces, n, 2)),
        dma((subs, 2)), dma((2 * max(DIRECT_IN, 1),)), dma((subs,)), dma((subs,)),
        dma((pieces,)), dma((pieces,)), dma((pieces,)), dma((pieces,)),
        dma((pieces,)), dma((pieces,)), dma((pieces,)), dma((pieces,)), dma((7,)),
    ]
    out = pl.pallas_call(
        functools.partial(kernel, n),
        out_shape=jax.ShapeDtypeStruct((x.shape[0], columns), BF16),
        in_specs=[hbm, hbm, vmem, hbm, hbm, vmem],
        out_specs=vmem,
        scratch_shapes=scratch,
        compiler_params=pltpu.CompilerParams(
            collective_id=0, has_side_effects=True, vmem_limit_bytes=56 * 2**20
        ),
    )(x, enc, enc_bias, dec, cross, dec_bias)
    return out[None]


def solution(mesh):
    placed = (
        P("layer", "seq", None),
        P("layer", "seq", "feat"),
        P("layer", "feat"),
        P("layer", "feat", "seq"),
        P("feat", ("layer", "seq")),
        P("layer", "feat"),
    )
    groups = mesh.shape["feat"]

    def body(mlp_inputs, *rest):
        fits = groups == LINE and mesh.shape["seq"] == LINE and mlp_inputs.shape[1] % (UNIT * groups) == 0
        if fits and mesh.shape["layer"] == 2 and rest[0].shape[2] % 256 == 0:
            return by_kernel(groups, mlp_inputs, *rest)
        return per_device(mlp_inputs, *rest)

    return jax.shard_map(
        body, mesh=mesh, in_specs=placed, out_specs=P("layer", "seq", "feat"), check_vma=False
    )
```

```python
import functools

import jax
import jax.numpy as jnp
from jax import lax
from jax.experimental import pallas as pl
from jax.experimental.pallas import tpu as pltpu
from jax.sharding import PartitionSpec as P

MESH = pl.DeviceIdType.MESH
F32, BF16 = jnp.float32, jnp.bfloat16


def passed_along(x, axis, by):
    devices = lax.axis_size(axis)
    pairs = [(i, i + by) for i in range(devices) if 0 <= i + by < devices]
    return lax.ppermute(x, axis, pairs)


def per_device(mlp_inputs, enc_weight, enc_bias, dec_weight, dec_cross, dec_bias):
    token_rows = mlp_inputs[0]
    layer_index = lax.axis_index("layer")
    pre_acts = jnp.dot(
        token_rows,
        lax.all_gather(enc_weight[0], "seq", axis=0, tiled=True),
        preferred_element_type=F32,
    )
    features = jnp.maximum(pre_acts + enc_bias[0], 0.0).astype(BF16)
    own_terms = jnp.dot(
        features,
        lax.all_gather(dec_weight[0], "seq", axis=1, tiled=True),
        preferred_element_type=F32,
    )
    half_rows = features.shape[0] // 2
    sent_half = passed_along(features[half_rows:], "layer", 1)
    cross_input = jnp.where(layer_index == 0, features[:half_rows], sent_half)
    cross_terms = jnp.dot(
        cross_input,
        lax.all_gather(dec_cross, ("layer", "seq"), axis=1, tiled=True),
        preferred_element_type=F32,
    )
    own_sums, cross_sums = (
        lax.psum_scatter(own_terms, "feat", scatter_dimension=1, tiled=True),
        lax.psum_scatter(cross_terms, "feat", scatter_dimension=1, tiled=True),
    )
    moved_sums = passed_along(cross_sums, "layer", 1)
    cross_full = jnp.concatenate([moved_sums, cross_sums], axis=0)
    total = own_sums + dec_bias[0] + jnp.where(layer_index == 1, cross_full, 0.0)
    return total.astype(BF16)[None]


UNIT = 16
LINE = 4
FINE_IN, FINE_OUT = 2, 2
DIRECT_IN, DIRECT_OUT = 0, 0
STEP_LAGS = {
    "own": 1.1, "forward": 2.2, "decode": 4.0, "sum": 3.5, "encode": -1.7, "edge_encode": -5.0,
}
FIRST_PIECE = ((0.01, 0.2), (0.1, 0.3), (0.6, 0.7))
SPREAD = 0.5


def decoded(features, columns):
    return lax.dot_general(features, columns, (((1,), (1,)), ((), ())), preferred_element_type=F32)


def cuts_of(s, steps):
    return 2 if s < FINE_IN or s >= steps - FINE_OUT else 1


def parts_of(steps):
    parts, start = [], []
    for s in range(steps):
        start.append(len(parts))
        parts += [(s, c, cuts_of(s, steps)) for c in range(cuts_of(s, steps))]
    return parts, start


def kernel(
    n, x_hbm, enc_hbm, encb_ref, dec_hbm, cross_hbm, decb_ref, out_ref,
    xv, enc_ref, dec_ref, cross_ref, xsend, xall, pf, psend, prec, drec, qsend, qrec, feats,
    oown, osend, orecv, csend, crecv, rsum, crs, fin, fcr,
    ld_sem, cw_r, x1_r, x2_r, p_r, d_r, q_r, g_r, o_r, c_r, f_r, h_r,
    x1_s, x2_s, f_s, h_s, sent,
):
    layer, f, z = lax.axis_index("layer"), lax.axis_index("feat"), lax.axis_index("seq")
    k = enc_ref.shape[0]
    half = cross_hbm.shape[0]
    r, width = xv.shape[0], enc_ref.shape[1]
    pieces = r // UNIT
    steps = pieces * n
    parts, start = parts_of(steps)
    mid = n // 2
    hrows = mid * UNIT
    first, second = layer == 0, layer == 1
    side = lax.div(z, mid)
    inner = (z == mid - 1) | (z == mid)
    edge = (z == 0) | (z == n - 1)
    z_edge, z_inner, z_other, z_far = side * (n - 1), mid - 1 + side, mid - side, (1 - side) * (n - 1)
    far = pl.ds(pl.multiple_of(side * hrows, hrows), hrows)
    near = pl.ds(pl.multiple_of((1 - side) * hrows, hrows), hrows)

    def peer(dx):
        total, bit = 0, 1
        while bit < n:
            own = lax.rem(lax.div(f, bit), 2)
            total = total + bit * ((1 - own) if dx & bit else own)
            bit *= 2
        return total

    sequence = [(0, dx) for dx in range(n)]
    sequence += [(u, dx) for u in range(1, pieces) for dx in range(n - 1, 0, -1)]
    sequence += [(u, 0) for u in range(1, pieces)]

    def split(s):
        return sequence[s]

    def outgoing(u, dx):
        return u * (n - 1) + dx - 1

    def cols(i):
        _, c, cuts = parts[i]
        return pl.ds(c * (width // cuts), width // cuts)

    def block(t):
        return pl.ds(pl.multiple_of(t * UNIT, UNIT), UNIT)

    def copy(src, dst, ss, rs, to):
        a, b, c = to
        return pltpu.make_async_remote_copy(
            src_ref=src, dst_ref=dst, send_sem=ss, recv_sem=rs,
            device_id={"layer": a, "feat": b, "seq": c}, device_id_type=MESH,
        )

    role = [None]

    def on(cond, run):
        if cond is None or (role[0] is not None and cond is role[0]):
            run()
        elif role[0] is not None and (cond is edge or cond is inner):
            return
        else:
            pl.when(cond)(run)

    def send(cond, make):
        on(cond, lambda: make().start())

    def arrive(cond, dst, sem):
        on(cond, lambda: copy(dst, dst, sem, sem, (layer, f, z)).wait_recv())

    def left(cond, src, sem):
        on(cond, lambda: copy(src, src, sem, sem, (layer, f, z)).wait_send())

    turns = [lax.rem(z + d, n) for d in (mid, mid + 1, mid - 1, 0)]
    S_P, S_Q, S_G, S_E, S_O, S_C, S_W = range(7)

    loads = [
        pltpu.make_async_copy(x_hbm.at[pl.ds(pl.multiple_of(f * r, UNIT), r)], xv, ld_sem.at[0]),
        pltpu.make_async_copy(enc_hbm, enc_ref, ld_sem.at[1]),
        pltpu.make_async_copy(cross_hbm, cross_ref.at[pl.ds(0, half)], ld_sem.at[2]),
        pltpu.make_async_copy(dec_hbm, dec_ref, ld_sem.at[3]),
    ]
    for load in loads:
        load.start()

    barrier = pltpu.get_barrier_semaphore()
    greeted = [(layer, f, lax.rem(z + a, n)) for a in range(1, n)]
    greeted += [(layer, lax.rem(f + a, n), z) for a in range(1, n)]
    greeted += [(1 - layer, lax.rem(f + a, n), z) for a in range(n)]
    for a, b, c in greeted:
        pl.semaphore_signal(
            barrier, inc=1, device_id={"layer": a, "feat": b, "seq": c}, device_id_type=MESH
        )

    loads[0].wait()
    for u in range(pieces):
        for t in range(n):
            xsend[u, t] = xv[u * UNIT:(u + 1) * UNIT, t * k:(t + 1) * k]
        if u == 0:
            pl.semaphore_wait(barrier, len(greeted))
        for d in range(n - 1, 0, -1):
            for sign in (1, -1):
                t = z + sign * d
                send((t < n) & (t >= 0), lambda t=t, u=u: copy(
                    xsend.at[u, t], xall.at[u, f, block(z)], x1_s.at[u], x1_r.at[u + 1 if u else lax.rem(side + lax.div(t, mid), 2)], (layer, f, t)))
        xall[u, f, block(z), :] = xsend[u, z]
    loads[2].wait()
    send(second, lambda: copy(
        cross_ref.at[pl.ds(0, half)], cross_ref.at[pl.ds(half, half)], sent.at[S_W], cw_r.at[0], (0, f, z)))

    halves = ((far, 0), (near, 1))
    whole = (pl.ds(0, 2 * hrows), 0)

    def spread_at(u, dx, h):
        return (dx - 1) * 2 + h if u == 0 else (u + 1) * (n - 1) + dx - 1

    def spread(u, half):
        part, h = half
        blocks = mid - 1 + h if u == 0 else n - 1
        arrive(None, xall.at[u, f, pl.ds(0, blocks * UNIT)], x1_r.at[u + 1 if u else h])
        for dx in range(1, n):
            send(None, lambda dx=dx: copy(
                xall.at[u, f, part], xall.at[u, f, part], x2_s.at[u], x2_r.at[spread_at(u, dx, h)],
                (layer, peer(dx), z)))

    def encode(s, chosen):
        u, dx = split(s)
        p = peer(dx)
        if dx:
            for part, h in chosen if u == 0 else (whole,):
                arrive(None, xall.at[u, p, part], x2_r.at[spread_at(u, dx, h)])
        rows = chosen[0][0] if len(chosen) == 1 else pl.ds(0, 2 * hrows)
        pf[s, rows] = jnp.dot(xall[u, p, rows], enc_ref[...], preferred_element_type=F32)

        def rounded():
            psend[s, rows] = pf[s, rows].astype(BF16)
        on(edge, rounded)
        for i in range(start[s], start[s] + cuts_of(s, steps)):
            for part, h in chosen:
                at = lambda i=i, part=part: psend.at[s, part, cols(i)]
                if h == 0 and s < DIRECT_IN:
                    send(edge, lambda i=i, at=at: copy(
                        at(), drec.at[s, :, cols(i)], sent.at[S_P], d_r.at[i], (layer, f, z_other)))
                else:
                    send(edge, lambda i=i, at=at, part=part, h=h: copy(
                        at(), prec.at[s, part, cols(i)], sent.at[S_P], p_r.at[i, h], (layer, f, z_inner)))

    def relay(i):
        s = parts[i][0]
        if s >= DIRECT_IN:
            arrive(inner, prec.at[s, far, cols(i)], p_r.at[i, 0])

        def passed():
            total = pf[s, far, cols(i)]
            if s >= DIRECT_IN:
                total += prec[s, far, cols(i)].astype(F32)
            qsend[s, :, cols(i)] = total.astype(BF16)
        on(inner, passed)
        send(inner, lambda: copy(
            qsend.at[s, :, cols(i)], qrec.at[s, :, cols(i)], sent.at[S_Q], q_r.at[i], (layer, f, z_other)))

    def own(i):
        s = parts[i][0]
        arrive(inner, prec.at[s, near, cols(i)], p_r.at[i, 1])
        if s < DIRECT_IN:
            arrive(inner, drec.at[s, :, cols(i)], d_r.at[i])
        arrive(inner, qrec.at[s, :, cols(i)], q_r.at[i])

        def activated():
            total = pf[s, near, cols(i)] + encb_ref[:, cols(i)]
            total += prec[s, near, cols(i)].astype(F32)
            total += qrec[s, :, cols(i)].astype(F32)
            if s < DIRECT_IN:
                total += drec[s, :, cols(i)].astype(F32)
            feats[s, near, cols(i)] = jnp.maximum(total, 0.0).astype(BF16)
        on(inner, activated)
        at = lambda: feats.at[s, near, cols(i)]
        to = [(g_r.at[i], S_G, z_other), (p_r.at[start[s], 0], S_E, z_edge)]
        if s >= steps - DIRECT_OUT:
            to = [(p_r.at[start[s], 0], S_E, z_far)] + to
        for sem, ss, zz in to:
            send(inner, lambda sem=sem, ss=ss, zz=zz: copy(at(), at(), sent.at[ss], sem, (layer, f, zz)))

    def forward(i):
        s = parts[i][0]
        at = lambda: feats.at[s, far, cols(i)]
        arrive(inner, at(), g_r.at[i])
        if s < steps - DIRECT_OUT:
            send(inner, lambda: copy(at(), at(), sent.at[S_E], p_r.at[start[s], 0], (layer, f, z_edge)))

    def decode(s):
        u, dx = split(s)
        arrive(edge, feats.at[s], p_r.at[start[s], 0])

        def crossed():
            @pl.when(first)
            def _():
                csend[u * n + dx] = decoded(feats[s], cross_ref[...]).astype(BF16)
            send(first, lambda: copy(
                csend.at[u * n + dx], crecv.at[u * n + dx], sent.at[S_C], c_r.at[u], (1, peer(dx), z)))

        if not dx:
            crossed()
        terms = decoded(feats[s], dec_ref[...])
        if dx:
            osend[outgoing(u, dx)] = terms.astype(BF16)
            send(None, lambda: copy(
                osend.at[outgoing(u, dx)], orecv.at[outgoing(u, dx)], sent.at[S_O], o_r.at[u], (layer, peer(dx), z)))
            crossed()
        else:
            oown[u] = terms

    def summed(u):
        arrive(None, orecv.at[pl.ds(u * (n - 1), n - 1)], o_r.at[u])
        total = oown[u]
        for dx in range(1, n):
            total += orecv[outgoing(u, dx)].astype(F32)
        rsum[u] = total.astype(BF16)
        for t in turns:
            here = (z == t) & (f == z)
            send(jnp.logical_not(here), lambda t=t: copy(
                rsum.at[u, block(t)], fin.at[u, f], f_s.at[u], f_r.at[u], (layer, z, t)))

        @pl.when(f == z)
        def _():
            fin[u, f] = rsum[u, block(z), :]

    def crossed_sum(u):
        arrive(second, crecv.at[pl.ds(u * n, n)], c_r.at[u])

        @pl.when(second)
        def _():
            sums = crecv[u * n].astype(F32)
            for i in range(1, n):
                sums += crecv[u * n + i].astype(F32)
            for h in range(2):
                crs[u, h] = sums[:, h * half:(h + 1) * half].astype(BF16)
        slot = lax.rem(z, 2) * n + f
        for h in range(2):
            to = h * mid + lax.div(z, 2)
            for t in turns:
                here = (z == t) & (f == to)
                send(second & jnp.logical_not(here), lambda h=h, t=t, to=to: copy(
                    crs.at[u, h, block(t)], fcr.at[u, slot],
                    h_s.at[u], h_r.at[u], (layer, to, t)))

            @pl.when(second & (f == to))
            def _(h=h):
                fcr[u, slot] = crs[u, h, block(z), :]

    own_rows = f == z
    own_cross = lax.rem(f, 2) == lax.div(z, 2)

    def each(run, u, mine, whole, other):
        count = whole.shape[1]
        run(mine, whole.at[u, pl.ds(0, count - 1)], other.at[u])
        rest = jnp.logical_not(mine) if mine is own_rows else second & jnp.logical_not(own_cross)
        run(rest, whole.at[u], other.at[u])

    def finish(u):
        each(arrive, u, own_rows, fin, f_r)
        each(arrive, u, second & own_cross, fcr, h_r)
        for g in range(n):
            part = slice(g * r + u * UNIT, g * r + (u + 1) * UNIT)

            @pl.when(first)
            def _():
                out_ref[part] = (fin[u, g].astype(F32) + decb_ref[...]).astype(BF16)

            @pl.when(second)
            def _():
                cross = jnp.concatenate([fcr[u, g].astype(F32), fcr[u, n + g].astype(F32)], axis=1)
                out_ref[part] = (fin[u, g].astype(F32) + cross + decb_ref[...]).astype(BF16)

    for h in range(2):
        spread(0, halves[h])
        if h == 0:
            loads[1].wait()
        encode(0, halves[h:h + 1])

    last = [max(s for s in range(steps) if split(s)[0] == u) for u in range(pieces)]

    def ordered(cond):
        events = []

        def place(time, rank, run, *given):
            events.append((time, rank, len(events), run, given))

        if cond is inner:
            for i, (s, c, cuts) in enumerate(parts):
                begin = s + c / cuts
                place(begin, 0, relay, i)
                place(begin + STEP_LAGS["own"], 1, own, i)
                place(begin + STEP_LAGS["forward"], 2, forward, i)
        for dx in range(1, n):
            for h in range(2):
                place(FIRST_PIECE[dx - 1][h], 3, encode, dx, halves[h:h + 1])
        for u in range(1, pieces):
            place(SPREAD * u, 3, spread, u, whole)
        decoded_at = []
        for s in range(steps):
            if s >= n:
                early = s + STEP_LAGS["encode"] if cond is inner else s + STEP_LAGS["edge_encode"]
                place(max(early, 1.05 + 0.3 * (s - n)), 3, encode, s, halves)
            time = s + STEP_LAGS["decode"]
            decoded_at.append(time)
            place(time, 4, decode, s)
        for u in range(pieces):
            late = decoded_at[last[u]] + (0 if u else STEP_LAGS["sum"])
            place(late, 5, summed, u)
            place(late if u == 0 else decoded_at[-1], 6, crossed_sum, u)
        place(steps - 2.5 + STEP_LAGS["decode"], 5, finish, 0)
        place(0.5, 6, loads[3].wait)
        place(0.5, 7, lambda: arrive(first, cross_ref.at[pl.ds(half, half)], cw_r.at[0]))
        return sorted(events, key=lambda e: e[:3])

    for cond in (edge, inner):
        @pl.when(cond)
        def _(cond=cond):
            role[0] = cond
            for _, _, _, run, given in ordered(cond):
                run(*given)
            role[0] = None
    for u in range(pieces - 1):
        if u:
            finish(u)
        left(None, xall.at[u, f, pl.ds(0, (n - 1) * UNIT)], x1_s.at[u])
        left(None, xall.at[u, pl.ds(0, n - 1)], x2_s.at[u])
        each(left, u, own_rows, fin, f_s)
        each(left, u, second & own_cross, fcr, h_s)
    u = pieces - 1
    left(None, xall.at[u, f, pl.ds(0, (n - 1) * UNIT)], x1_s.at[u])
    left(None, xall.at[u, pl.ds(0, n - 1)], x2_s.at[u])
    left(edge, psend, sent.at[S_P])
    left(inner, qsend, sent.at[S_Q])
    left(inner, qsend, sent.at[S_G])
    left(inner, feats, sent.at[S_E])
    left(None, osend.at[pl.ds(0, steps - pieces)], sent.at[S_O])
    left(first, csend, sent.at[S_C])
    left(second, cross_ref.at[pl.ds(0, half)], sent.at[S_W])
    finish(u)
    each(left, u, own_rows, fin, f_s)
    each(left, u, second & own_cross, fcr, h_s)


def by_kernel(n, mlp_inputs, enc_weight, enc_bias, dec_weight, dec_cross, dec_bias):
    x, enc, dec, cross = mlp_inputs[0], enc_weight[0], dec_weight[0].T, dec_cross.T
    r = x.shape[0] // n
    k, width = enc.shape
    columns, half = dec.shape[0], cross.shape[0]
    pieces = r // UNIT
    steps, rows = pieces * n, n * UNIT
    subs = len(parts_of(steps)[0])
    vmem = pl.BlockSpec(memory_space=pltpu.VMEM)
    hbm = pl.BlockSpec(memory_space=pl.ANY)
    dma = pltpu.SemaphoreType.DMA
    scratch = [
        pltpu.VMEM((r, x.shape[1]), BF16),
        pltpu.VMEM(enc.shape, BF16),
        pltpu.VMEM(dec.shape, BF16),
        pltpu.VMEM((2 * half, width), BF16),
        pltpu.VMEM((pieces, n, UNIT, k), BF16),
        pltpu.VMEM((pieces, n, rows, k), BF16),
        pltpu.VMEM((steps, rows, width), F32),
        pltpu.VMEM((steps, rows, width), BF16),
        pltpu.VMEM((steps, rows, width), BF16),
        pltpu.VMEM((max(DIRECT_IN, 1), rows // 2, width), BF16),
        pltpu.VMEM((steps, rows // 2, width), BF16),
        pltpu.VMEM((steps, rows // 2, width), BF16),
        pltpu.VMEM((steps, rows, width), BF16),
        pltpu.VMEM((pieces, rows, columns), F32),
        pltpu.VMEM((steps, rows, columns), BF16),
        pltpu.VMEM((steps, rows, columns), BF16),
        pltpu.VMEM((steps, rows, 2 * half), BF16),
        pltpu.VMEM((steps, rows, 2 * half), BF16),
        pltpu.VMEM((pieces, rows, columns), BF16),
        pltpu.VMEM((pieces, 2, rows, half), BF16),
        pltpu.VMEM((pieces, n, UNIT, columns), BF16),
        pltpu.VMEM((pieces, 2 * n, UNIT, half), BF16),
        dma((4,)), dma((1,)), dma((pieces + 1,)), dma(((pieces + 1) * (n - 1),)),
        dma((subs, 2)), dma((max(2 * DIRECT_IN, 1),)), dma((subs,)), dma((subs,)),
        dma((pieces,)), dma((pieces,)), dma((pieces,)), dma((pieces,)),
        dma((pieces,)), dma((pieces,)), dma((pieces,)), dma((pieces,)), dma((7,)),
    ]
    out = pl.pallas_call(
        functools.partial(kernel, n),
        out_shape=jax.ShapeDtypeStruct((x.shape[0], columns), BF16),
        in_specs=[hbm, hbm, vmem, hbm, hbm, vmem],
        out_specs=vmem,
        scratch_shapes=scratch,
        compiler_params=pltpu.CompilerParams(
            collective_id=0, has_side_effects=True, vmem_limit_bytes=56 * 2**20
        ),
    )(x, enc, enc_bias, dec, cross, dec_bias)
    return out[None]


def solution(mesh):
    placed = (
        P("layer", "seq", None),
        P("layer", "seq", "feat"),
        P("layer", "feat"),
        P("layer", "feat", "seq"),
        P("feat", ("layer", "seq")),
        P("layer", "feat"),
    )
    groups = mesh.shape["feat"]

    def body(mlp_inputs, *rest):
        fits = groups == LINE and mesh.shape["seq"] == LINE and mlp_inputs.shape[1] % (UNIT * groups) == 0
        if fits and mesh.shape["layer"] == 2 and rest[0].shape[2] % 256 == 0:
            return by_kernel(groups, mlp_inputs, *rest)
        return per_device(mlp_inputs, *rest)

    return jax.shard_map(
        body, mesh=mesh, in_specs=placed, out_specs=P("layer", "seq", "feat"), check_vma=False
    )
```
